768 devices in a mesh: grp: 8 (over x, core), blk: 96 (over y, z).
Axes of the slice: x: 4, y: 8, z: 12, core: 2. Of those that a mesh axis runs over, the one named last changes fastest.
Arguments:
- fine_pops: float32 [8, 19, 1536, 256], P('grp', None, 'blk'), may hold values from 0.38 to 8.7, as said below
- fine_solid: float32 [8, 1536, 256], P('grp', 'blk'), may hold values from 0.05 to 0.6
- coarse_pops: float32 [8, 19, 768, 256], P('grp', None, 'blk'), may hold values from 0.38 to 8.7, as said below
- coarse_solid: float32 [8, 768, 256], P('grp', 'blk'), may hold values from 0.05 to 0.6
- coarse_slot: int32 [8], replicated, may hold values from 0 to 31, as said below
Outputs:
- fine_out: float32 [8, 19, 1536, 256], P('grp', None, 'blk')
- coarse_out: float32 [8, 19, 768, 256], P('grp', None, 'blk')
The draws below stay inside these ranges and needn't reach their ends.
Inputs may be any that keep to these rules, and one draw needn't show every extreme that they name: `fine_pops`: each population is between 0.7 and 1.3 times 20 w_i. `coarse_pops`: each population is between 0.7 and 1.3 times 20 w_i. `coarse_slot`: the 8 entries are distinct, and 31 is one of them.
All inputs are finite; a program needn't handle non-finite values.
Results may differ from the reference program's by a relative error of at most 0.0001.
Values sent between devices are 32-bit elements; how exact they have to be, the bound alone decides.
A program may use at most 128 MiB of HBM per device.

```python
import jax
import jax.numpy as jnp
import numpy as np
from jax import lax

BX = 16
ZB = 1
GROUPS = 8
FX = 1536
CX = 768
CELLS = 256


def weight_column():
    return jnp.array([1.0 / 3.0] + [1.0 / 18.0] * 6 + [1.0 / 36.0] * 12, jnp.float32)[None, :, None, None]


def draw_fine_pops(key, part):
    shape = (GROUPS, 19, FX, CELLS)
    jitter = jax.random.uniform(key, shape, jnp.float32, -0.3, 0.3)
    return 20.0 * weight_column() * (1.0 + jitter)


def draw_coarse_pops(key, part):
    shape = (GROUPS, 19, CX, CELLS)
    jitter = jax.random.uniform(key, shape, jnp.float32, -0.3, 0.3)
    return 20.0 * weight_column() * (1.0 + jitter)


def draw_coarse_slot(key, part):
    leading = jax.random.permutation(jax.random.fold_in(key, 11), 4 * GROUPS - 1)[:GROUPS - 1].astype(jnp.int32)
    codes = jnp.concatenate([leading, jnp.array([4 * GROUPS - 1], jnp.int32)])
    order = jax.random.permutation(jax.random.fold_in(key, 12), GROUPS)
    return codes[order].astype(jnp.int32)


def levels(rng, shape, split, smallest, top_value):
    def one(dim, blocks):
        draws = jax.random.uniform(jax.random.fold_in(jax.random.fold_in(rng, 6), dim), (blocks,), jnp.float32, smallest / len(split), top_value / len(split))
        return jnp.repeat(jnp.exp(draws), shape[dim] // blocks).reshape((-1,) + (1,) * (len(shape) - dim - 1))

    level = one(*split[0])
    for cut in split[1:]:
        level = level * one(*cut)
    return level


def setup_inputs(seed: int = 0) -> dict:
    seeds = jax.random.split(jax.random.key(seed), 6)
    fine_pops = draw_fine_pops(jax.random.fold_in(seeds[5], 71), 0)
    fine_solid = jnp.clip(0.05 + 0.55 * jax.random.uniform(seeds[1], (GROUPS, FX, CELLS), jnp.float32) ** levels(seeds[1], (GROUPS, FX, CELLS), ((0, 8), (1, 96)), -0.2, 0.2), 0.05, 0.6)
    coarse_pops = draw_coarse_pops(jax.random.fold_in(seeds[5], 71), 0)
    coarse_solid = jnp.clip(0.05 + 0.55 * jax.random.uniform(seeds[3], (GROUPS, CX, CELLS), jnp.float32) ** levels(seeds[3], (GROUPS, CX, CELLS), ((0, 8), (1, 96)), -0.2, 0.2), 0.05, 0.6)
    coarse_slot = draw_coarse_slot(jax.random.fold_in(seeds[5], 71), 0)
    return dict(fine_pops=fine_pops, fine_solid=fine_solid, coarse_pops=coarse_pops, coarse_solid=coarse_solid, coarse_slot=coarse_slot)


lattice_vel = np.array([[0, 0, 0], [1, 0, 0], [-1, 0, 0], [0, 1, 0], [0, -1, 0], [0, 0, 1], [0, 0, -1], [1, 1, 0], [-1, -1, 0], [1, -1, 0], [-1, 1, 0], [1, 0, 1], [-1, 0, -1], [1, 0, -1], [-1, 0, 1], [0, 1, 1], [0, -1, -1], [0, 1, -1], [0, -1, 1]])
lattice_weight = np.array([1.0 / 3.0] + [1.0 / 18.0] * 6 + [1.0 / 36.0] * 12)
opposite_index = [0, 2, 1, 4, 3, 6, 5, 8, 7, 10, 9, 12, 11, 14, 13, 16, 15, 18, 17]
tau_fine = 0.6
tau_coarse = 0.55


def spread_table(table, populations):
    return jnp.asarray(table, populations.dtype).reshape((19,) + (1,) * (populations.ndim - 1))


def equilibrium(populations):
    density = jnp.sum(populations, axis=0)
    velocity = [jnp.sum(spread_table(lattice_vel[:, k], populations) * populations, axis=0) / density for k in range(3)]
    projected = spread_table(lattice_vel[:, 0], populations) * velocity[0]
    projected = projected + spread_table(lattice_vel[:, 1], populations) * velocity[1]
    projected = projected + spread_table(lattice_vel[:, 2], populations) * velocity[2]
    speed_sq = velocity[0] * velocity[0] + velocity[1] * velocity[1] + velocity[2] * velocity[2]
    return spread_table(lattice_weight, populations) * density * (1.0 + 3.0 * projected + 4.5 * projected * projected - 1.5 * speed_sq)


def collide_cells(populations, solid, relax):
    equil = equilibrium(populations)
    mirrored = jnp.stack([populations[j] for j in opposite_index])
    return populations - (1.0 - solid) * (populations - equil) / relax + solid * (mirrored - populations)


def stream_periodic(collided):
    return jnp.stack([jnp.roll(collided[j], (int(lattice_vel[j, 0]), int(lattice_vel[j, 1]), int(lattice_vel[j, 2])), axis=(0, 1, 2)) for j in range(19)])


def restrict_block(populations):
    shape = populations.shape
    averaged = populations.reshape(19, shape[1] // 2, 2, shape[2] // 2, 2, shape[3] // 2, 2).mean(axis=(2, 4, 6))
    equil = equilibrium(averaged)
    return equil + (2.0 * tau_coarse / tau_fine) * (averaged - equil)


def reference(fine_pops, fine_solid, coarse_pops, coarse_solid, coarse_slot):
    zlength = BX * ZB

    def fine_group(arrays):
        populations, solid = arrays
        populations = populations.reshape(19, FX, BX, zlength)
        solid = solid.reshape(FX, BX, zlength)
        for substep in range(2):
            populations = stream_periodic(collide_cells(populations, solid, tau_fine))
        return populations

    fine_new = lax.map(fine_group, (fine_pops, fine_solid))
    restricted = lax.map(restrict_block, fine_new)
    half_y = BX // 2
    half_z = zlength // 2
    outputs = []
    for group in range(GROUPS):
        populations = coarse_pops[group].reshape(19, CX, BX, zlength)
        for quadrant in range(4):
            matched = coarse_slot == group * 4 + quadrant
            source = jnp.argmax(matched.astype(jnp.int32)).astype(jnp.int32)
            matched_tile = restricted[source]
            low_y = (quadrant // 2) * half_y
            low_z = (quadrant % 2) * half_z
            region = populations[:, :, low_y:low_y + half_y, low_z:low_z + half_z]
            populations = populations.at[:, :, low_y:low_y + half_y, low_z:low_z + half_z].set(jnp.where(jnp.any(matched), matched_tile, region))
        solid = coarse_solid[group].reshape(CX, BX, zlength)
        populations = stream_periodic(collide_cells(populations, solid, tau_coarse))
        outputs.append(populations.reshape(19, CX, BX * zlength))
    return fine_new.reshape(GROUPS, 19, FX, BX * zlength), jnp.stack(outputs)
```

```python
import jax
import jax.numpy as jnp
import numpy as np
from jax import lax
from jax.experimental import pallas as pl
from jax.experimental.pallas import tpu as pltpu
from jax.sharding import PartitionSpec as P

MESH = pl.DeviceIdType.MESH
F32 = jnp.float32

lattice_vel = [
    (0, 0, 0), (1, 0, 0), (-1, 0, 0), (0, 1, 0), (0, -1, 0), (0, 0, 1), (0, 0, -1),
    (1, 1, 0), (-1, -1, 0), (1, -1, 0), (-1, 1, 0), (1, 0, 1), (-1, 0, -1),
    (1, 0, -1), (-1, 0, 1), (0, 1, 1), (0, -1, -1), (0, 1, -1), (0, -1, 1),
]
tau_fine = 0.6
tau_coarse = 0.55
rescale = 2.0 * tau_coarse / tau_fine
RIGHT = [i for i in range(19) if lattice_vel[i][0] == 1]
LEFT = [i for i in range(19) if lattice_vel[i][0] == -1]
STAY = [i for i in range(19) if lattice_vel[i][0] == 0]
X = 16
C = 8
PAD = 8
HALVES = (0, 128)


def relaxed(f, keep_even, keep_odd, a):
    even = [None] * 19
    odd = [None] * 19
    for i in range(1, 19, 2):
        even[i] = f[i] + f[i + 1]
        odd[i] = f[i] - f[i + 1]
    rho = f[0]
    for i in range(1, 19, 2):
        rho = rho + even[i]
    j = []
    for axis in range(3):
        total = None
        for i in range(1, 19, 2):
            c = lattice_vel[i][axis]
            if c:
                term = odd[i]
                if total is None:
                    total = term if c > 0 else -term
                else:
                    total = total + term if c > 0 else total - term
        j.append(total)
    inverse = 1.0 / rho
    q = a * inverse
    jj = j[0] * j[0] + j[1] * j[1] + j[2] * j[2]
    base = a * rho - (1.5 * q) * jj
    out = [None] * 19
    out[0] = 2.0 * keep_even * f[0] + (1.0 / 3.0) * base
    axis_base = (1.0 / 18.0) * base
    edge_base = (1.0 / 36.0) * base
    axis_q = (4.5 / 18.0) * q
    edge_q = (4.5 / 36.0) * q
    axis_a = (3.0 / 18.0) * a
    edge_a = (3.0 / 36.0) * a
    for i in range(1, 19, 2):
        cj = None
        for axis in range(3):
            c = lattice_vel[i][axis]
            if c:
                if cj is None:
                    cj = j[axis] if c > 0 else -j[axis]
                else:
                    cj = cj + j[axis] if c > 0 else cj - j[axis]
        if i < 7:
            e = axis_base + axis_q * (cj * cj) + keep_even * even[i]
            o = axis_a * cj + keep_odd * odd[i]
        else:
            e = edge_base + edge_q * (cj * cj) + keep_even * even[i]
            o = edge_a * cj + keep_odd * odd[i]
        out[i] = e + o
        out[i + 1] = e - o
    return out


def collide(f, solid, tau):
    a = (1.0 - solid) * (1.0 / tau)
    keep_even = 0.5 * (1.0 - a)
    return relaxed(f, keep_even, keep_even - solid, a)


def lane_shift(low, high, cy, cz, lane):
    if cy == 0 and cz == 0:
        return low, high
    shift = 16 * cy + cz
    parts = []
    for v in (low, high):
        moved = pltpu.roll(v, shift % 128, 1)
        if cz:
            wrapped = pltpu.roll(v, (shift - 16 * cz) % 128, 1)
            z = lane % 16
            moved = jnp.where(z == (0 if cz > 0 else 15), wrapped, moved)
        parts.append(moved)
    if cy == 0:
        return parts[0], parts[1]
    crossing = lane < 16 if cy > 0 else lane >= 112
    return jnp.where(crossing, parts[1], parts[0]), jnp.where(crossing, parts[0], parts[1])


def lanes(rows):
    return lax.broadcasted_iota(jnp.int32, (rows, 128), 1)


def streamed(source, row, rows):
    lane = lanes(rows)
    low, high = [], []
    for i in range(19):
        cx, cy, cz = lattice_vel[i]
        start = row - cx
        a = source[i, start : start + rows, 0:128]
        b = source[i, start : start + rows, 128:256]
        a, b = lane_shift(a, b, cy, cz, lane)
        low.append(a)
        high.append(b)
    return low, high


def kernel(
    groups, blocks, slot_ref, fine_hbm, solid_hbm, coarse_hbm, csolid_hbm, fine_out, coarse_out,
    fine, solid, coarse, csolid, first, second, moved, averaged, boxes, paste, settled, cmoved,
    to_right, to_left, from_left, from_right, cto_right, cto_left, cfrom_left, cfrom_right,
    load_sem, store_sem, halo_send, halo_recv, box_send, box_recv, chalo_send, chalo_recv,
):
    g = lax.axis_index("grp")
    b = lax.axis_index("blk")
    right = (g, lax.rem(b + 1, blocks))
    left = (g, lax.rem(b + blocks - 1, blocks))
    peers = [(lax.rem(g + d, groups), b) for d in range(1, groups)]

    loads = [
        pltpu.make_async_copy(fine_hbm.at[0], fine, load_sem.at[0]),
        pltpu.make_async_copy(solid_hbm.at[0], solid.at[PAD : PAD + X], load_sem.at[1]),
        pltpu.make_async_copy(coarse_hbm.at[0], coarse, load_sem.at[2]),
        pltpu.make_async_copy(csolid_hbm.at[0], csolid, load_sem.at[3]),
    ]
    for load in loads:
        load.start()
    barrier = pltpu.get_barrier_semaphore()
    for device in [left, right] + peers:
        pl.semaphore_signal(barrier, inc=1, device_id=device, device_id_type=MESH)

    row = lax.broadcasted_iota(jnp.int32, (256, 128), 0)
    column = lax.broadcasted_iota(jnp.int32, (256, 128), 1)
    hit = (row // 32 == column // 16) & ((row % 16) // 2 == column % 8)
    boxes[...] = jnp.where(hit, 0.125, 0.0).astype(jnp.bfloat16)

    loads[0].wait()
    loads[1].wait()
    for t in range(X // 8):
        for h in HALVES:
            span = slice(h, h + 128)
            f = [fine[i, 8 * t : 8 * t + 8, span] for i in range(19)]
            s = solid[PAD + 8 * t : PAD + 8 * t + 8, span]
            f = collide(f, s, tau_fine)
            for i in range(19):
                first[i, PAD + 8 * t : PAD + 8 * t + 8, span] = f[i]
            if t == 0:
                for k, i in enumerate(LEFT):
                    to_left[k : k + 1, span] = f[i][1:2]
                for k, i in enumerate(LEFT + STAY):
                    to_left[5 + k : 6 + k, span] = f[i][0:1]
                to_left[19:20, span] = s[0:1]
            if t == X // 8 - 1:
                for k, i in enumerate(RIGHT):
                    to_right[k : k + 1, span] = f[i][6:7]
                for k, i in enumerate(RIGHT + STAY):
                    to_right[5 + k : 6 + k, span] = f[i][7:8]
                to_right[19:20, span] = s[7:8]

    pl.semaphore_wait(barrier, groups + 1)
    halos = [
        pltpu.make_async_remote_copy(
            to_right, from_left, halo_send.at[0], halo_recv.at[0], right, MESH),
        pltpu.make_async_remote_copy(
            to_left, from_right, halo_send.at[1], halo_recv.at[1], left, MESH),
    ]
    for halo in halos:
        halo.start()

    def second_collision(start, rows):
        low, high = streamed(first, start, rows)
        for f, h in ((low, 0), (high, 128)):
            span = slice(h, h + 128)
            f = collide(f, solid[start : start + rows, span], tau_fine)
            for i in range(19):
                second[i, start : start + rows, span] = f[i]

    def second_stream(start, rows):
        low, high = streamed(second, start, rows)
        for i in range(19):
            moved[0, i, start - PAD : start - PAD + rows, :] = low[i]
            moved[1, i, start - PAD : start - PAD + rows, :] = high[i]

    for t in range(X // 8):
        second_collision(PAD + 8 * t, 8)
    for t in range(X // 8):
        second_stream(PAD + 8 * t, 8)

    for halo in halos:
        halo.wait_recv()
    for k, i in enumerate(RIGHT):
        first[i, PAD - 2 : PAD - 1, :] = from_left[k : k + 1, :]
    for k, i in enumerate(RIGHT + STAY):
        first[i, PAD - 1 : PAD, :] = from_left[5 + k : 6 + k, :]
    solid[PAD - 1 : PAD, :] = from_left[19:20, :]
    for k, i in enumerate(LEFT):
        first[i, PAD + X + 1 : PAD + X + 2, :] = from_right[k : k + 1, :]
    for k, i in enumerate(LEFT + STAY):
        first[i, PAD + X : PAD + X + 1, :] = from_right[5 + k : 6 + k, :]
    solid[PAD + X : PAD + X + 1, :] = from_right[19:20, :]
    second_collision(PAD - 1, 2)
    second_collision(PAD + X - 1, 2)
    second_stream(PAD, 2)
    second_stream(PAD + X - 2, 2)
    stores = [
        pltpu.make_async_copy(moved.at[k], fine_out.at[0, :, :, h : h + 128], store_sem.at[k])
        for k, h in enumerate(HALVES)
    ]
    for store in stores:
        store.start()

    for i in range(19):
        for k, h in enumerate(HALVES):
            averaged[8 * i : 8 * i + 8, h : h + 128] = (
                moved[k, i, pl.ds(0, 8, stride=2), :] + moved[k, i, pl.ds(1, 8, stride=2), :])
    rest = averaged[...]
    total = None
    for part in range(3):
        piece = rest.astype(jnp.bfloat16)
        product = jnp.dot(piece, boxes[...], preferred_element_type=F32)
        total = product if total is None else total + product
        if part < 2:
            rest = rest - piece.astype(F32)
    a = jnp.full((8, 128), 1.0 - rescale, F32)
    keep = jnp.full((8, 128), 0.5 * rescale, F32)
    f = relaxed([total[8 * i : 8 * i + 8] for i in range(19)], keep, keep, a)
    lane = lanes(8)
    near = lane % 16 < 8
    for k in range(10):
        paste[g, k] = jnp.where(near, f[2 * k], f[min(2 * k + 1, 18)])
    sends = []
    for d, peer in enumerate(peers):
        sends.append(pltpu.make_async_remote_copy(
            paste.at[g], paste.at[g], box_send.at[d], box_recv.at[g], peer, MESH))
    for send in sends:
        send.start()

    loads[2].wait()
    loads[3].wait()
    sources, present = [], []
    for q in range(4):
        source = jnp.int32(0)
        found = jnp.int32(0)
        for k in range(groups):
            match = (slot_ref[k] == 4 * g + q).astype(jnp.int32)
            source = jnp.maximum(source, k * match)
            found = jnp.maximum(found, match)
        sources.append(source)
        present.append(found)
    for d, peer in enumerate(peers):
        pltpu.make_async_remote_copy(
            paste.at[peer[0]], paste.at[peer[0]], box_send.at[d], box_recv.at[peer[0]], peer, MESH
        ).wait_recv()
    for half, h in enumerate(HALVES):
        span = slice(h, h + 128)
        one, two = sources[2 * half], sources[2 * half + 1]
        put = jnp.where(
            near,
            jnp.full((8, 128), present[2 * half], jnp.int32),
            jnp.full((8, 128), present[2 * half + 1], jnp.int32),
        ) > 0
        f = []
        for k in range(10):
            tile_one, tile_two = paste[one, k], paste[two, k]
            i = 2 * k
            value = jnp.where(near, tile_one, pltpu.roll(tile_two, 8, 1))
            f.append(jnp.where(put, value, coarse[i, :, span]))
            if i + 1 < 19:
                value = jnp.where(near, pltpu.roll(tile_one, 120, 1), tile_two)
                f.append(jnp.where(put, value, coarse[i + 1, :, span]))
        f = collide(f, csolid[:, span], tau_coarse)
        for i in range(19):
            settled[i, PAD : PAD + C, span] = f[i]
        for k, i in enumerate(LEFT):
            cto_left[k : k + 1, span] = f[i][0:1]
        for k, i in enumerate(RIGHT):
            cto_right[k : k + 1, span] = f[i][7:8]
    chalos = [
        pltpu.make_async_remote_copy(
            cto_right, cfrom_left, chalo_send.at[0], chalo_recv.at[0], right, MESH),
        pltpu.make_async_remote_copy(
            cto_left, cfrom_right, chalo_send.at[1], chalo_recv.at[1], left, MESH),
    ]
    for halo in chalos:
        halo.start()
    for halo in chalos:
        halo.wait_recv()
    for k, i in enumerate(RIGHT):
        settled[i, PAD - 1 : PAD, :] = cfrom_left[k : k + 1, :]
    for k, i in enumerate(LEFT):
        settled[i, PAD + C : PAD + C + 1, :] = cfrom_right[k : k + 1, :]
    low, high = streamed(settled, PAD, C)
    for i in range(19):
        cmoved[i, :, 0:128] = low[i]
        cmoved[i, :, 128:256] = high[i]
    stores.append(pltpu.make_async_copy(cmoved, coarse_out.at[0], store_sem.at[2]))
    stores[2].start()
    for copy in halos + sends + chalos:
        copy.wait_send()
    for store in stores:
        store.wait()


def solution(mesh):
    groups, blocks = mesh.shape["grp"], mesh.shape["blk"]

    def per_device(fine_pops, fine_solid, coarse_pops, coarse_solid, coarse_slot):
        body = lambda *refs: kernel(groups, blocks, *refs)
        return pl.pallas_call(
            body,
            out_shape=(
                jax.ShapeDtypeStruct(fine_pops.shape, F32),
                jax.ShapeDtypeStruct(coarse_pops.shape, F32),
            ),
            in_specs=[pl.BlockSpec(memory_space=pltpu.SMEM)]
            + [pl.BlockSpec(memory_space=pl.ANY)] * 4,
            out_specs=(pl.BlockSpec(memory_space=pl.ANY), pl.BlockSpec(memory_space=pl.ANY)),
            scratch_shapes=[
                pltpu.VMEM((19, X, 256), F32),
                pltpu.VMEM((X + 2 * PAD, 256), F32),
                pltpu.VMEM((19, C, 256), F32),
                pltpu.VMEM((C, 256), F32),
                pltpu.VMEM((19, X + 2 * PAD, 256), F32),
                pltpu.VMEM((19, X + 2 * PAD, 256), F32),
                pltpu.VMEM((2, 19, X, 128), F32),
                pltpu.VMEM((19 * 8, 256), F32),
                pltpu.VMEM((256, 128), jnp.bfloat16),
                pltpu.VMEM((groups, 10, 8, 128), F32),
                pltpu.VMEM((19, C + 2 * PAD, 256), F32),
                pltpu.VMEM((19, C, 256), F32),
                pltpu.VMEM((24, 256), F32),
                pltpu.VMEM((24, 256), F32),
                pltpu.VMEM((24, 256), F32),
                pltpu.VMEM((24, 256), F32),
                pltpu.VMEM((8, 256), F32),
                pltpu.VMEM((8, 256), F32),
                pltpu.VMEM((8, 256), F32),
                pltpu.VMEM((8, 256), F32),
                pltpu.SemaphoreType.DMA((4,)),
                pltpu.SemaphoreType.DMA((3,)),
                pltpu.SemaphoreType.DMA((2,)),
                pltpu.SemaphoreType.DMA((2,)),
                pltpu.SemaphoreType.DMA((groups,)),
                pltpu.SemaphoreType.DMA((groups,)),
                pltpu.SemaphoreType.DMA((2,)),
                pltpu.SemaphoreType.DMA((2,)),
            ],
            compiler_params=pltpu.CompilerParams(collective_id=0, has_side_effects=True),
        )(coarse_slot, fine_pops, fine_solid, coarse_pops, coarse_solid)

    placed = (
        P("grp", None, "blk", None),
        P("grp", "blk", None),
        P("grp", None, "blk", None),
        P("grp", "blk", None),
        P(),
    )
    return jax.shard_map(
        per_device,
        mesh=mesh,
        in_specs=placed,
        out_specs=(P("grp", None, "blk", None), P("grp", None, "blk", None)),
        check_vma=False,
    )
```

```python
import jax
import jax.numpy as jnp
import numpy as np
from jax import lax
from jax.experimental import pallas as pl
from jax.experimental.pallas import tpu as pltpu
from jax.sharding import PartitionSpec as P

MESH = pl.DeviceIdType.MESH
F32 = jnp.float32

lattice_vel = [
    (0, 0, 0), (1, 0, 0), (-1, 0, 0), (0, 1, 0), (0, -1, 0), (0, 0, 1), (0, 0, -1),
    (1, 1, 0), (-1, -1, 0), (1, -1, 0), (-1, 1, 0), (1, 0, 1), (-1, 0, -1),
    (1, 0, -1), (-1, 0, 1), (0, 1, 1), (0, -1, -1), (0, 1, -1), (0, -1, 1),
]
tau_fine = 0.6
tau_coarse = 0.55
rescale = 2.0 * tau_coarse / tau_fine
RIGHT = [i for i in range(19) if lattice_vel[i][0] == 1]
LEFT = [i for i in range(19) if lattice_vel[i][0] == -1]
STAY = [i for i in range(19) if lattice_vel[i][0] == 0]
X = 16
C = 8
PAD = 8
HALVES = (0, 128)


def relaxed(f, keep_even, keep_odd, a):
    even = [None] * 19
    odd = [None] * 19
    for i in range(1, 19, 2):
        even[i] = f[i] + f[i + 1]
        odd[i] = f[i] - f[i + 1]
    rho = f[0]
    for i in range(1, 19, 2):
        rho = rho + even[i]
    j = []
    for axis in range(3):
        total = None
        for i in range(1, 19, 2):
            c = lattice_vel[i][axis]
            if c:
                term = odd[i]
                if total is None:
                    total = term if c > 0 else -term
                else:
                    total = total + term if c > 0 else total - term
        j.append(total)
    inverse = 1.0 / rho
    q = a * inverse
    jj = j[0] * j[0] + j[1] * j[1] + j[2] * j[2]
    base = a * rho - (1.5 * q) * jj
    out = [None] * 19
    out[0] = 2.0 * keep_even * f[0] + (1.0 / 3.0) * base
    axis_base = (1.0 / 18.0) * base
    edge_base = (1.0 / 36.0) * base
    axis_q = (4.5 / 18.0) * q
    edge_q = (4.5 / 36.0) * q
    axis_a = (3.0 / 18.0) * a
    edge_a = (3.0 / 36.0) * a
    for i in range(1, 19, 2):
        cj = None
        for axis in range(3):
            c = lattice_vel[i][axis]
            if c:
                if cj is None:
                    cj = j[axis] if c > 0 else -j[axis]
                else:
                    cj = cj + j[axis] if c > 0 else cj - j[axis]
        if i < 7:
            e = axis_base + axis_q * (cj * cj) + keep_even * even[i]
            o = axis_a * cj + keep_odd * odd[i]
        else:
            e = edge_base + edge_q * (cj * cj) + keep_even * even[i]
            o = edge_a * cj + keep_odd * odd[i]
        out[i] = e + o
        out[i + 1] = e - o
    return out


def collide(f, solid, tau):
    a = (1.0 - solid) * (1.0 / tau)
    keep_even = 0.5 * (1.0 - a)
    return relaxed(f, keep_even, keep_even - solid, a)


def lane_shift(low, high, cy, cz, lane):
    if cy == 0 and cz == 0:
        return low, high
    shift = 16 * cy + cz
    parts = []
    for v in (low, high):
        moved = pltpu.roll(v, shift % 128, 1)
        if cz:
            wrapped = pltpu.roll(v, (shift - 16 * cz) % 128, 1)
            z = lane % 16
            moved = jnp.where(z == (0 if cz > 0 else 15), wrapped, moved)
        parts.append(moved)
    if cy == 0:
        return parts[0], parts[1]
    crossing = lane < 16 if cy > 0 else lane >= 112
    return jnp.where(crossing, parts[1], parts[0]), jnp.where(crossing, parts[0], parts[1])


def lanes(rows):
    return lax.broadcasted_iota(jnp.int32, (rows, 128), 1)


def streamed(source, row, rows):
    lane = lanes(rows)
    low, high = [], []
    for i in range(19):
        cx, cy, cz = lattice_vel[i]
        start = row - cx
        a = source[i, start : start + rows, 0:128]
        b = source[i, start : start + rows, 128:256]
        a, b = lane_shift(a, b, cy, cz, lane)
        low.append(a)
        high.append(b)
    return low, high


def kernel(
    groups, blocks, slot_ref, fine_hbm, solid_hbm, coarse_hbm, csolid_hbm, moved, settled,
    fine, solid, coarse, csolid, first, second, edge, boxes, inner, outer_r, outer_l,
    to_right, to_left, from_left, from_right, cto_right, cto_left, cfrom_left, cfrom_right,
    load_sem, ready, halo_send, halo_recv, chalo_send, chalo_recv, box_send, box_recv,
):
    g = lax.axis_index("grp")
    b = lax.axis_index("blk")
    right = (g, lax.rem(b + 1, blocks))
    left = (g, lax.rem(b + blocks - 1, blocks))
    peers = [(lax.rem(g + d, groups), b) for d in (4, 3, 5, 2, 6, 1, 7)]

    loads = [
        pltpu.make_async_copy(solid_hbm.at[0], solid.at[PAD : PAD + X], load_sem.at[0]),
        pltpu.make_async_copy(fine_hbm.at[0, :, 8:16], fine.at[:, 8:16], load_sem.at[1]),
        pltpu.make_async_copy(fine_hbm.at[0, :, 0:8], fine.at[:, 0:8], load_sem.at[2]),
        pltpu.make_async_copy(csolid_hbm.at[0], csolid.at[PAD : PAD + C], load_sem.at[3]),
        pltpu.make_async_copy(coarse_hbm.at[0], coarse.at[:, PAD : PAD + C], load_sem.at[4]),
    ]
    for load in loads:
        load.start()
    barrier = pltpu.get_barrier_semaphore()
    for device in [left] + peers:
        pl.semaphore_signal(barrier, inc=1, device_id=device, device_id_type=MESH)

    def first_collision(t):
        out = []
        for h in HALVES:
            span = slice(h, h + 128)
            f = [fine[i, 8 * t : 8 * t + 8, span] for i in range(19)]
            f = collide(f, solid[PAD + 8 * t : PAD + 8 * t + 8, span], tau_fine)
            for i in range(19):
                first[i, PAD + 8 * t : PAD + 8 * t + 8, span] = f[i]
            out.append(f)
        return out

    loads[0].wait()
    loads[1].wait()
    for f, h in zip(first_collision(1), HALVES):
        span = slice(h, h + 128)
        for k, i in enumerate(RIGHT + STAY):
            to_right[4 * k : 4 * k + 4, span] = f[i][4:8]
        to_right[56:60, span] = solid[PAD + 12 : PAD + 16, span]
        for k, i in enumerate(LEFT):
            to_right[60 + 2 * k : 62 + 2 * k, span] = f[i][6:8]
    pl.semaphore_wait(barrier, groups)
    halo_r = pltpu.make_async_remote_copy(
        to_right, from_left, halo_send.at[0], halo_recv.at[0], right, MESH)
    halo_r.start()
    pl.semaphore_signal(ready, inc=1, device_id=right, device_id_type=MESH)

    loads[2].wait()
    for f, h in zip(first_collision(0), HALVES):
        span = slice(h, h + 128)
        for k, i in enumerate(LEFT + STAY):
            to_left[4 * k : 4 * k + 4, span] = f[i][0:4]
        to_left[56:60, span] = solid[PAD : PAD + 4, span]
        for k, i in enumerate(RIGHT):
            to_left[60 + 2 * k : 62 + 2 * k, span] = f[i][0:2]

    loads[3].wait()
    loads[4].wait()
    for h in HALVES:
        span = slice(h, h + 128)
        s = csolid[PAD : PAD + C, span]
        f = collide([coarse[i, PAD : PAD + C, span] for i in range(19)], s, tau_coarse)
        for k in range(5):
            cto_left[k : k + 1, span] = f[LEFT[k]][0:1]
            cto_right[k : k + 1, span] = f[RIGHT[k]][C - 1 : C]
        cto_left[5:6, span] = s[0:1]
        cto_right[5:6, span] = s[C - 1 : C]
    chalo_r = pltpu.make_async_remote_copy(
        cto_right, cfrom_left, chalo_send.at[0], chalo_recv.at[0], right, MESH)
    chalo_r.start()

    row = lax.broadcasted_iota(jnp.int32, (256, 128), 0)
    column = lax.broadcasted_iota(jnp.int32, (256, 128), 1)
    hit = (row // 32 == column // 16) & ((row % 16) // 2 == column % 8)
    boxes[...] = jnp.where(hit, 0.125, 0.0).astype(jnp.bfloat16)

    def second_collision(start, rows):
        low, high = streamed(first, start, rows)
        for f, h in ((low, 0), (high, 128)):
            span = slice(h, h + 128)
            f = collide(f, solid[start : start + rows, span], tau_fine)
            for i in range(19):
                second[i, start : start + rows, span] = f[i]

    def box_means(pair_sums):
        rest, parts = pair_sums, []
        for _ in range(3):
            piece = rest.astype(jnp.bfloat16).astype(F32)
            parts.append(piece)
            rest = rest - piece
        stacked = jnp.concatenate(parts, axis=0).astype(jnp.bfloat16)
        product = jnp.dot(stacked, boxes[...], preferred_element_type=F32)
        n = pair_sums.shape[0]
        return product[:n] + product[n : 2 * n] + product[2 * n :]

    def rescaled(means, rows):
        a = jnp.full((rows, 128), 1.0 - rescale, F32)
        keep = jnp.full((rows, 128), 0.5 * rescale, F32)
        return relaxed([means[rows * i : rows * i + rows] for i in range(19)], keep, keep, a)

    def near(rows):
        return lanes(rows) % 16 < 8

    def deliver(which, buffer):
        sends = []
        for d, peer in enumerate(peers):
            sends.append(pltpu.make_async_remote_copy(
                buffer.at[g], buffer.at[g], box_send.at[which, d], box_recv.at[which, g],
                peer, MESH))
        for send in sends:
            send.start()
        return sends

    def collect(which, buffer):
        for d, peer in enumerate(peers):
            pltpu.make_async_remote_copy(
                buffer.at[peer[0]], buffer.at[peer[0]], box_send.at[which, d],
                box_recv.at[which, peer[0]], peer, MESH).wait_recv()

    for t in range(X // 8):
        second_collision(PAD + 8 * t, 8)
    for t in range(X // 8):
        low, high = streamed(second, PAD + 8 * t, 8)
        for i in range(19):
            moved[0, X * i + 8 * t : X * i + 8 * t + 8, :] = low[i]
            moved[1, X * i + 8 * t : X * i + 8 * t + 8, :] = high[i]
    sums = [
        moved[k, pl.ds(0, 152, stride=2), :] + moved[k, pl.ds(1, 152, stride=2), :]
        for k in range(2)
    ]
    f = rescaled(box_means(jnp.concatenate(sums, axis=1)), 8)
    for k in range(10):
        inner[g, k] = jnp.where(near(8), f[2 * k], f[min(2 * k + 1, 18)])
    sends = deliver(0, inner)

    pl.semaphore_wait(ready, 1)
    halo_l = pltpu.make_async_remote_copy(
        to_left, from_right, halo_send.at[1], halo_recv.at[1], left, MESH)
    halo_l.start()
    chalo_l = pltpu.make_async_remote_copy(
        cto_left, cfrom_right, chalo_send.at[1], chalo_recv.at[1], left, MESH)
    chalo_l.start()

    def outer_planes(side, outer):
        if side:
            low, high = streamed(second, PAD + X - 2, 4)
        else:
            low, high = streamed(second, PAD - 2, 4)
        for k, values in enumerate((low, high)):
            for i in range(19):
                edge[side, k, 4 * i : 4 * i + 4, :] = values[i]
                if side:
                    moved[k, X * i + X - 2 : X * i + X, :] = values[i][0:2]
                else:
                    moved[k, X * i : X * i + 2, :] = values[i][2:4]
        sums = [
            edge[side, k, pl.ds(0, 40, stride=2), :] + edge[side, k, pl.ds(1, 40, stride=2), :]
            for k in range(2)
        ]
        f = rescaled(box_means(jnp.concatenate(sums, axis=1)), 2)
        for k in range(10):
            outer[g, 2 * k : 2 * k + 2, :] = jnp.where(near(2), f[2 * k], f[min(2 * k + 1, 18)])

    halo_l.wait_recv()
    top = PAD + X
    for k, i in enumerate(LEFT + STAY):
        first[i, top : top + 4, :] = from_right[4 * k : 4 * k + 4, :]
    for k, i in enumerate(RIGHT):
        first[i, top : top + 2, :] = from_right[60 + 2 * k : 62 + 2 * k, :]
    solid[top : top + 4, :] = from_right[56:60, :]
    second_collision(top - 1, 4)
    outer_planes(1, outer_r)
    sends += deliver(1, outer_r)

    halo_r.wait_recv()
    for k, i in enumerate(RIGHT + STAY):
        first[i, PAD - 4 : PAD, :] = from_left[4 * k : 4 * k + 4, :]
    for k, i in enumerate(LEFT):
        first[i, PAD - 2 : PAD, :] = from_left[60 + 2 * k : 62 + 2 * k, :]
    solid[PAD - 4 : PAD, :] = from_left[56:60, :]
    second_collision(PAD - 3, 4)
    outer_planes(0, outer_l)
    sends += deliver(2, outer_l)

    sources, present = [], []
    for q in range(4):
        source = jnp.int32(0)
        found = jnp.int32(0)
        for k in range(groups):
            match = (slot_ref[k] == 4 * g + q).astype(jnp.int32)
            source = jnp.maximum(source, k * match)
            found = jnp.maximum(found, match)
        sources.append(source)
        present.append(found)

    def pasted(half, rows, tile, start):
        span = slice(128 * half, 128 * half + 128)
        one, two = sources[2 * half], sources[2 * half + 1]
        close = near(rows)
        put = jnp.where(
            close,
            jnp.full((rows, 128), present[2 * half], jnp.int32),
            jnp.full((rows, 128), present[2 * half + 1], jnp.int32),
        ) > 0
        f = []
        for k in range(10):
            tile_one, tile_two = tile(one, k), tile(two, k)
            i = 2 * k
            value = jnp.where(close, tile_one, pltpu.roll(tile_two, 8, 1))
            f.append(jnp.where(put, value, coarse[i, start : start + rows, span]))
            if i + 1 < 19:
                value = jnp.where(close, pltpu.roll(tile_one, 120, 1), tile_two)
                f.append(jnp.where(put, value, coarse[i + 1, start : start + rows, span]))
        return collide(f, csolid[start : start + rows, span], tau_coarse), put, span

    collect(0, inner)
    for half in range(2):
        f, _, span = pasted(half, C, lambda source, k: inner[source, k], PAD)
        for i in range(19):
            settled[i, PAD : PAD + C, span] = f[i]

    chalo_l.wait_recv()
    csolid[PAD + C : PAD + C + 1, :] = cfrom_right[5:6, :]
    collect(1, outer_r)
    for half in range(2):
        f, put, span = pasted(
            half, 2, lambda source, k: outer_r[source, 2 * k : 2 * k + 2, :], PAD + C - 1)
        for i in range(19):
            settled[i, PAD + C - 1 : PAD + C, span] = f[i][0:1]
        for k, i in enumerate(LEFT):
            settled[i, PAD + C : PAD + C + 1, span] = jnp.where(
                put[1:2], f[i][1:2], cfrom_right[k : k + 1, span])

    chalo_r.wait_recv()
    csolid[PAD - 1 : PAD, :] = cfrom_left[5:6, :]
    collect(2, outer_l)
    for half in range(2):
        f, put, span = pasted(
            half, 2, lambda source, k: outer_l[source, 2 * k : 2 * k + 2, :], PAD - 1)
        for i in range(19):
            settled[i, PAD : PAD + 1, span] = f[i][1:2]
        for k, i in enumerate(RIGHT):
            settled[i, PAD - 1 : PAD, span] = jnp.where(
                put[0:1], f[i][0:1], cfrom_left[k : k + 1, span])

    for copy in [halo_r, halo_l, chalo_r, chalo_l] + sends:
        copy.wait_send()


def finish(moved, settled, fine_out, coarse_out, cmoved, store_sem):
    stores = [
        pltpu.make_async_copy(moved.at[k], fine_out.at[0, :, :, h : h + 128], store_sem.at[k])
        for k, h in enumerate(HALVES)
    ]
    for store in stores:
        store.start()
    low, high = streamed(settled, PAD, C)
    for i in range(19):
        cmoved[i, :, 0:128] = low[i]
        cmoved[i, :, 128:256] = high[i]
    stores.append(pltpu.make_async_copy(cmoved, coarse_out.at[0], store_sem.at[2]))
    stores[2].start()
    for store in stores:
        store.wait()


def solution(mesh):
    groups, blocks = mesh.shape["grp"], mesh.shape["blk"]
    vmem = pl.BlockSpec(memory_space=pltpu.VMEM)
    hbm = pl.BlockSpec(memory_space=pltpu.HBM)

    def per_device(fine_pops, fine_solid, coarse_pops, coarse_solid, coarse_slot):
        body = lambda *refs: kernel(groups, blocks, *refs)
        moved, settled = pl.pallas_call(
            body,
            out_shape=(
                jax.ShapeDtypeStruct((2, 19 * X, 128), F32),
                jax.ShapeDtypeStruct((19, C + 2 * PAD, 256), F32),
            ),
            in_specs=[pl.BlockSpec(memory_space=pltpu.SMEM)] + [hbm] * 4,
            out_specs=(vmem, vmem),
            scratch_shapes=[
                pltpu.VMEM((19, X, 256), F32),
                pltpu.VMEM((X + 2 * PAD, 256), F32),
                pltpu.VMEM((19, C + 2 * PAD, 256), F32),
                pltpu.VMEM((C + 2 * PAD, 256), F32),
                pltpu.VMEM((19, X + 2 * PAD, 256), F32),
                pltpu.VMEM((19, X + 2 * PAD, 256), F32),
                pltpu.VMEM((2, 2, 80, 128), F32),
                pltpu.VMEM((256, 128), jnp.bfloat16),
                pltpu.VMEM((groups, 10, 8, 128), F32),
                pltpu.VMEM((groups, 24, 128), F32),
                pltpu.VMEM((groups, 24, 128), F32),
            ]
            + [pltpu.VMEM((72, 256), F32)] * 4
            + [pltpu.VMEM((8, 256), F32)] * 4
            + [
                pltpu.SemaphoreType.DMA((5,)),
                pltpu.SemaphoreType.REGULAR,
                pltpu.SemaphoreType.DMA((2,)),
                pltpu.SemaphoreType.DMA((2,)),
                pltpu.SemaphoreType.DMA((2,)),
                pltpu.SemaphoreType.DMA((2,)),
                pltpu.SemaphoreType.DMA((3, groups)),
                pltpu.SemaphoreType.DMA((3, groups)),
            ],
            compiler_params=pltpu.CompilerParams(
                collective_id=0, has_side_effects=True, vmem_limit_bytes=16 << 20),
        )(coarse_slot, *[
            pltpu.with_memory_space_constraint(x, pltpu.HBM)
            for x in (fine_pops, fine_solid, coarse_pops, coarse_solid)
        ])
        return pl.pallas_call(
            finish,
            out_shape=(
                jax.ShapeDtypeStruct(fine_pops.shape, F32),
                jax.ShapeDtypeStruct(coarse_pops.shape, F32),
            ),
            in_specs=[vmem, vmem],
            out_specs=(hbm, hbm),
            scratch_shapes=[pltpu.VMEM((19, C, 256), F32), pltpu.SemaphoreType.DMA((3,))],
            compiler_params=pltpu.CompilerParams(vmem_limit_bytes=4 << 20),
        )(moved.reshape(2, 19, X, 128), settled)

    placed = (
        P("grp", None, "blk", None),
        P("grp", "blk", None),
        P("grp", None, "blk", None),
        P("grp", "blk", None),
        P(),
    )
    return jax.shard_map(
        per_device,
        mesh=mesh,
        in_specs=placed,
        out_specs=(P("grp", None, "blk", None), P("grp", None, "blk", None)),
        check_vma=False,
    )
```

```python
import jax
import jax.numpy as jnp
import numpy as np
from jax import lax
from jax.experimental import pallas as pl
from jax.experimental.pallas import tpu as pltpu
from jax.sharding import PartitionSpec as P

MESH = pl.DeviceIdType.MESH
F32 = jnp.float32

lattice_vel = [
    (0, 0, 0), (1, 0, 0), (-1, 0, 0), (0, 1, 0), (0, -1, 0), (0, 0, 1), (0, 0, -1),
    (1, 1, 0), (-1, -1, 0), (1, -1, 0), (-1, 1, 0), (1, 0, 1), (-1, 0, -1),
    (1, 0, -1), (-1, 0, 1), (0, 1, 1), (0, -1, -1), (0, 1, -1), (0, -1, 1),
]
tau_fine = 0.6
tau_coarse = 0.55
rescale = 2.0 * tau_coarse / tau_fine
RIGHT = [i for i in range(19) if lattice_vel[i][0] == 1]
LEFT = [i for i in range(19) if lattice_vel[i][0] == -1]
STAY = [i for i in range(19) if lattice_vel[i][0] == 0]
X = 16
C = 8
ROW = 12
PAD = 8
HALVES = (0, 128)


def relaxed(f, keep_even, keep_odd, a):
    even = [None] * 19
    odd = [None] * 19
    for i in range(1, 19, 2):
        even[i] = f[i] + f[i + 1]
        odd[i] = f[i] - f[i + 1]
    rho = f[0]
    for i in range(1, 19, 2):
        rho = rho + even[i]
    j = []
    for axis in range(3):
        total = None
        for i in range(1, 19, 2):
            c = lattice_vel[i][axis]
            if c:
                term = odd[i]
                if total is None:
                    total = term if c > 0 else -term
                else:
                    total = total + term if c > 0 else total - term
        j.append(total)
    inverse = 1.0 / rho
    q = a * inverse
    jj = j[0] * j[0] + j[1] * j[1] + j[2] * j[2]
    base = a * rho - (1.5 * q) * jj
    out = [None] * 19
    out[0] = 2.0 * keep_even * f[0] + (1.0 / 3.0) * base
    axis_base = (1.0 / 18.0) * base
    edge_base = (1.0 / 36.0) * base
    axis_q = (4.5 / 18.0) * q
    edge_q = (4.5 / 36.0) * q
    axis_a = (3.0 / 18.0) * a
    edge_a = (3.0 / 36.0) * a
    for i in range(1, 19, 2):
        cj = None
        for axis in range(3):
            c = lattice_vel[i][axis]
            if c:
                if cj is None:
                    cj = j[axis] if c > 0 else -j[axis]
                else:
                    cj = cj + j[axis] if c > 0 else cj - j[axis]
        if i < 7:
            e = axis_base + axis_q * (cj * cj) + keep_even * even[i]
            o = axis_a * cj + keep_odd * odd[i]
        else:
            e = edge_base + edge_q * (cj * cj) + keep_even * even[i]
            o = edge_a * cj + keep_odd * odd[i]
        out[i] = e + o
        out[i + 1] = e - o
    return out


def collide(f, solid, tau):
    a = (1.0 - solid) * (1.0 / tau)
    keep_even = 0.5 * (1.0 - a)
    return relaxed(f, keep_even, keep_even - solid, a)


def lane_shift(low, high, cy, cz, lane):
    if cy == 0 and cz == 0:
        return low, high
    shift = 16 * cy + cz
    parts = []
    for v in (low, high):
        moved = pltpu.roll(v, shift % 128, 1)
        if cz:
            wrapped = pltpu.roll(v, (shift - 16 * cz) % 128, 1)
            z = lane % 16
            moved = jnp.where(z == (0 if cz > 0 else 15), wrapped, moved)
        parts.append(moved)
    if cy == 0:
        return parts[0], parts[1]
    crossing = lane < 16 if cy > 0 else lane >= 112
    return jnp.where(crossing, parts[1], parts[0]), jnp.where(crossing, parts[0], parts[1])


def lanes(rows):
    return lax.broadcasted_iota(jnp.int32, (rows, 128), 1)


def streamed(source, row, rows):
    lane = lanes(rows)
    low, high = [], []
    for i in range(19):
        cx, cy, cz = lattice_vel[i]
        start = row - cx
        a = source[i, start : start + rows, 0:128]
        b = source[i, start : start + rows, 128:256]
        a, b = lane_shift(a, b, cy, cz, lane)
        low.append(a)
        high.append(b)
    return low, high


def kernel(
    groups, blocks, slot_hbm, fine_hbm, solid_hbm, coarse_hbm, csolid_hbm,
    fine_view, solid_view, coarse_view, csolid_view, moved, settled,
    fine, solid, coarse, csolid, first, second, edge, boxes, inner, outer_r, outer_l,
    from_left, from_right, sol_left, sol_right, cfrom_left, cfrom_right, csol_left, csol_right,
    slot_ref, load_sem, ready, lefts, peers_in, halo_send, halo_recv, box_send, box_recv,
):
    g = lax.axis_index("grp")
    b = lax.axis_index("blk")
    right = (g, lax.rem(b + 1, blocks))
    left = (g, lax.rem(b + blocks - 1, blocks))
    peers = [(lax.rem(g + d, groups), b) for d in (4, 3, 5, 2, 6, 1, 7)]

    late = lax.rem(b, ROW) == ROW - 1
    follows = lax.rem(b, ROW) == 0

    barrier = pltpu.get_barrier_semaphore()
    pl.semaphore_signal(barrier, inc=1, device_id=left, device_id_type=MESH)

    @pl.when(jnp.logical_not(late))
    def _():
        for device in peers:
            pl.semaphore_signal(barrier, inc=1, device_id=device, device_id_type=MESH)

    loads = [
        pltpu.make_async_copy(solid_hbm.at[0], solid.at[PAD : PAD + X], load_sem.at[0]),
        pltpu.make_async_copy(fine_hbm.at[0], fine, load_sem.at[1]),
        pltpu.make_async_copy(csolid_hbm.at[0], csolid.at[PAD : PAD + C], load_sem.at[2]),
        pltpu.make_async_copy(coarse_hbm.at[0], coarse.at[:, PAD : PAD + C], load_sem.at[3]),
        pltpu.make_async_copy(slot_hbm, slot_ref, load_sem.at[4]),
    ]

    def halo(k, source, target, device):
        return pltpu.make_async_remote_copy(
            source, target, halo_send.at[k], halo_recv.at[k], device, MESH)

    halos_r = [
        halo(0, fine_view.at[:, 1, :, 4:8], from_left, right),
        halo(1, solid_view.at[1, :, 4:8], sol_left, right),
        halo(2, coarse_view.at[:, :, C - 1 : C], cfrom_left, right),
        halo(3, csolid_view.at[:, C - 1 : C], csol_left, right),
    ]
    halos_l = [
        halo(4, fine_view.at[:, 0, :, 0:4], from_right, left),
        halo(5, solid_view.at[0, :, 0:4], sol_right, left),
        halo(6, coarse_view.at[:, :, 0:1], cfrom_right, left),
        halo(7, csolid_view.at[:, 0:1], csol_right, left),
    ]
    pl.semaphore_wait(barrier, jnp.where(late, 1, groups))
    for copy in halos_r:
        copy.start()
    pl.semaphore_signal(ready, inc=1, device_id=right, device_id_type=MESH)
    for load in loads:
        load.start()

    def first_collision(f, s, start, rows, span):
        f = collide(f, s, tau_fine)
        for i in range(19):
            first[i, start : start + rows, span] = f[i]

    row = lax.broadcasted_iota(jnp.int32, (256, 128), 0)
    column = lax.broadcasted_iota(jnp.int32, (256, 128), 1)
    hit = (row // 32 == column // 16) & ((row % 16) // 2 == column % 8)
    boxes[...] = jnp.where(hit, 0.125, 0.0).astype(jnp.bfloat16)

    def second_collision(start, rows):
        low, high = streamed(first, start, rows)
        for f, h in ((low, 0), (high, 128)):
            span = slice(h, h + 128)
            f = collide(f, solid[start : start + rows, span], tau_fine)
            for i in range(19):
                second[i, start : start + rows, span] = f[i]

    def box_means(pair_sums):
        rest, parts = pair_sums, []
        for _ in range(3):
            piece = rest.astype(jnp.bfloat16).astype(F32)
            parts.append(piece)
            rest = rest - piece
        stacked = jnp.concatenate(parts, axis=0).astype(jnp.bfloat16)
        product = jnp.dot(stacked, boxes[...], preferred_element_type=F32)
        n = pair_sums.shape[0]
        return product[:n] + product[n : 2 * n] + product[2 * n :]

    def rescaled(means, rows):
        a = jnp.full((rows, 128), 1.0 - rescale, F32)
        keep = jnp.full((rows, 128), 0.5 * rescale, F32)
        return relaxed([means[rows * i : rows * i + rows] for i in range(19)], keep, keep, a)

    def near(rows):
        return lanes(rows) % 16 < 8

    def messages(which, buffer):
        return [
            pltpu.make_async_remote_copy(
                buffer.at[g], buffer.at[g], box_send.at[which, d], box_recv.at[which, g],
                peer, MESH)
            for d, peer in enumerate(peers)
        ]

    sends = [messages(0, inner), messages(1, outer_r), messages(2, outer_l)]

    def deliver(which):
        for send in sends[which]:
            send.start()

    def collect(which, buffer):
        for d, peer in enumerate(peers):
            pltpu.make_async_remote_copy(
                buffer.at[peer[0]], buffer.at[peer[0]], box_send.at[which, d],
                box_recv.at[which, peer[0]], peer, MESH).wait_recv()

    loads[0].wait()
    loads[1].wait()
    for t in range(X // 8):
        for h in HALVES:
            span = slice(h, h + 128)
            first_collision(
                [fine[i, 8 * t : 8 * t + 8, span] for i in range(19)],
                solid[PAD + 8 * t : PAD + 8 * t + 8, span], PAD + 8 * t, 8, span)
    for t in range(X // 8):
        second_collision(PAD + 8 * t, 8)
    for t in range(X // 8):
        low, high = streamed(second, PAD + 8 * t, 8)
        for i in range(19):
            moved[0, X * i + 8 * t : X * i + 8 * t + 8, :] = low[i]
            moved[1, X * i + 8 * t : X * i + 8 * t + 8, :] = high[i]
    sums = [
        moved[k, pl.ds(0, 152, stride=2), :] + moved[k, pl.ds(1, 152, stride=2), :]
        for k in range(2)
    ]
    f = rescaled(box_means(jnp.concatenate(sums, axis=1)), 8)
    for k in range(10):
        inner[g, k] = jnp.where(near(8), f[2 * k], f[min(2 * k + 1, 18)])

    @pl.when(jnp.logical_not(late))
    def _():
        deliver(0)

    pl.semaphore_wait(ready, 1)
    for copy in halos_l:
        copy.start()

    @pl.when(follows)
    def _():
        for device in peers:
            pl.semaphore_signal(lefts, inc=1, device_id=device, device_id_type=MESH)

    def beyond(halo, halo_solid, start):
        for k, h in enumerate(HALVES):
            span = slice(h, h + 128)
            s = halo_solid[k, :, 0, :]
            solid[start : start + 4, span] = s
            first_collision([halo[i, k, :, 0, :] for i in range(19)], s, start, 4, span)

    def outer_planes(side, outer):
        if side:
            low, high = streamed(second, PAD + X - 2, 4)
        else:
            low, high = streamed(second, PAD - 2, 4)
        for k, values in enumerate((low, high)):
            for i in range(19):
                edge[side, k, 4 * i : 4 * i + 4, :] = values[i]
                if side:
                    moved[k, X * i + X - 2 : X * i + X, :] = values[i][0:2]
                else:
                    moved[k, X * i : X * i + 2, :] = values[i][2:4]
        sums = [
            edge[side, k, pl.ds(0, 40, stride=2), :] + edge[side, k, pl.ds(1, 40, stride=2), :]
            for k in range(2)
        ]
        f = rescaled(box_means(jnp.concatenate(sums, axis=1)), 2)
        for k in range(10):
            outer[g, 2 * k : 2 * k + 2, :] = jnp.where(near(2), f[2 * k], f[min(2 * k + 1, 18)])

    halos_l[0].wait_recv()
    halos_l[1].wait_recv()
    beyond(from_right, sol_right, PAD + X)
    second_collision(PAD + X - 1, 4)
    outer_planes(1, outer_r)

    @pl.when(jnp.logical_not(late))
    def _():
        deliver(1)

    @pl.when(follows)
    def _():
        pl.semaphore_wait(lefts, groups - 1)
        pl.semaphore_signal(peers_in, inc=1, device_id=left, device_id_type=MESH)

    halos_r[0].wait_recv()
    halos_r[1].wait_recv()
    beyond(from_left, sol_left, PAD - 4)
    second_collision(PAD - 3, 4)
    outer_planes(0, outer_l)

    @pl.when(late)
    def _():
        pl.semaphore_wait(peers_in, 1)
        deliver(0)
        deliver(1)

    deliver(2)

    loads[4].wait()
    sources, present = [], []
    for q in range(4):
        source = jnp.int32(0)
        found = jnp.int32(0)
        for k in range(groups):
            match = (slot_ref[k] == 4 * g + q).astype(jnp.int32)
            source = jnp.maximum(source, k * match)
            found = jnp.maximum(found, match)
        sources.append(source)
        present.append(found)

    def pasted(half, rows, tile, start):
        span = slice(128 * half, 128 * half + 128)
        one, two = sources[2 * half], sources[2 * half + 1]
        close = near(rows)
        put = jnp.where(
            close,
            jnp.full((rows, 128), present[2 * half], jnp.int32),
            jnp.full((rows, 128), present[2 * half + 1], jnp.int32),
        ) > 0
        f = []
        for k in range(10):
            tile_one, tile_two = tile(one, k), tile(two, k)
            i = 2 * k
            value = jnp.where(close, tile_one, pltpu.roll(tile_two, 8, 1))
            f.append(jnp.where(put, value, coarse[i, start : start + rows, span]))
            if i + 1 < 19:
                value = jnp.where(close, pltpu.roll(tile_one, 120, 1), tile_two)
                f.append(jnp.where(put, value, coarse[i + 1, start : start + rows, span]))
        return collide(f, csolid[start : start + rows, span], tau_coarse), span

    def cbeyond(halo, halo_solid, start):
        for k, h in enumerate(HALVES):
            span = slice(h, h + 128)
            csolid[start : start + 1, span] = halo_solid[k, :, 0, :]
            for i in range(19):
                coarse[i, start : start + 1, span] = halo[i, k, :, 0, :]

    loads[2].wait()
    loads[3].wait()
    halos_l[2].wait_recv()
    halos_l[3].wait_recv()
    cbeyond(cfrom_right, csol_right, PAD + C)
    collect(0, inner)
    for half in range(2):
        f, span = pasted(half, C, lambda source, k: inner[source, k], PAD)
        for i in range(19):
            settled[i, PAD : PAD + C, span] = f[i]

    collect(1, outer_r)
    for half in range(2):
        f, span = pasted(
            half, 2, lambda source, k: outer_r[source, 2 * k : 2 * k + 2, :], PAD + C - 1)
        for i in range(19):
            settled[i, PAD + C - 1 : PAD + C + 1, span] = f[i]

    halos_r[2].wait_recv()
    halos_r[3].wait_recv()
    cbeyond(cfrom_left, csol_left, PAD - 1)
    collect(2, outer_l)
    for half in range(2):
        f, span = pasted(
            half, 2, lambda source, k: outer_l[source, 2 * k : 2 * k + 2, :], PAD - 1)
        for i in range(19):
            settled[i, PAD - 1 : PAD + 1, span] = f[i]

    for copy in halos_r + halos_l + sends[0] + sends[1] + sends[2]:
        copy.wait_send()


def finish(moved, settled, fine_out, coarse_out, cmoved, store_sem):
    stores = [
        pltpu.make_async_copy(moved.at[k], fine_out.at[0, :, :, h : h + 128], store_sem.at[k])
        for k, h in enumerate(HALVES)
    ]
    for store in stores:
        store.start()
    low, high = streamed(settled, PAD, C)
    for i in range(19):
        cmoved[i, :, 0:128] = low[i]
        cmoved[i, :, 128:256] = high[i]
    stores.append(pltpu.make_async_copy(cmoved, coarse_out.at[0], store_sem.at[2]))
    stores[2].start()
    for store in stores:
        store.wait()


def solution(mesh):
    groups, blocks = mesh.shape["grp"], mesh.shape["blk"]
    vmem = pl.BlockSpec(memory_space=pltpu.VMEM)
    hbm = pl.BlockSpec(memory_space=pltpu.HBM)

    def planes(x, *leading):
        n = len(leading)
        order = tuple(range(n)) + (n + 1, n, n + 2)
        x = x.reshape(leading + (8, 2, 128)).transpose(order)
        return x.reshape(leading + (2, 8, 1, 128))

    def per_device(fine_pops, fine_solid, coarse_pops, coarse_solid, coarse_slot):
        body = lambda *refs: kernel(groups, blocks, *refs)
        moved, settled = pl.pallas_call(
            body,
            out_shape=(
                jax.ShapeDtypeStruct((2, 19 * X, 128), F32),
                jax.ShapeDtypeStruct((19, C + 2 * PAD, 256), F32),
            ),
            in_specs=[hbm] * 9,
            out_specs=(vmem, vmem),
            scratch_shapes=[
                pltpu.VMEM((19, X, 256), F32),
                pltpu.VMEM((X + 2 * PAD, 256), F32),
                pltpu.VMEM((19, C + 2 * PAD, 256), F32),
                pltpu.VMEM((C + 2 * PAD, 256), F32),
                pltpu.VMEM((19, X + 2 * PAD, 256), F32),
                pltpu.VMEM((19, X + 2 * PAD, 256), F32),
                pltpu.VMEM((2, 2, 80, 128), F32),
                pltpu.VMEM((256, 128), jnp.bfloat16),
                pltpu.VMEM((groups, 10, 8, 128), F32),
                pltpu.VMEM((groups, 24, 128), F32),
                pltpu.VMEM((groups, 24, 128), F32),
            ]
            + [pltpu.VMEM((19, 2, 4, 1, 128), F32)] * 2
            + [pltpu.VMEM((2, 4, 1, 128), F32)] * 2
            + [pltpu.VMEM((19, 2, 1, 1, 128), F32)] * 2
            + [pltpu.VMEM((2, 1, 1, 128), F32)] * 2
            + [
                pltpu.SMEM((groups,), jnp.int32),
                pltpu.SemaphoreType.DMA((5,)),
                pltpu.SemaphoreType.REGULAR,
                pltpu.SemaphoreType.REGULAR,
                pltpu.SemaphoreType.REGULAR,
                pltpu.SemaphoreType.DMA((8,)),
                pltpu.SemaphoreType.DMA((8,)),
                pltpu.SemaphoreType.DMA((3, groups)),
                pltpu.SemaphoreType.DMA((3, groups)),
            ],
            compiler_params=pltpu.CompilerParams(
                collective_id=0, has_side_effects=True, vmem_limit_bytes=16 << 20),
        )(*[
            pltpu.with_memory_space_constraint(x, pltpu.HBM)
            for x in (
                coarse_slot, fine_pops, fine_solid, coarse_pops, coarse_solid,
                planes(fine_pops, 19, 2), planes(fine_solid, 2),
                planes(coarse_pops, 19), planes(coarse_solid),
            )
        ])
        return pl.pallas_call(
            finish,
            out_shape=(
                jax.ShapeDtypeStruct(fine_pops.shape, F32),
                jax.ShapeDtypeStruct(coarse_pops.shape, F32),
            ),
            in_specs=[vmem, vmem],
            out_specs=(hbm, hbm),
            scratch_shapes=[pltpu.VMEM((19, C, 256), F32), pltpu.SemaphoreType.DMA((3,))],
            compiler_params=pltpu.CompilerParams(vmem_limit_bytes=4 << 20),
        )(moved.reshape(2, 19, X, 128), settled)

    placed = (
        P("grp", None, "blk", None),
        P("grp", "blk", None),
        P("grp", None, "blk", None),
        P("grp", "blk", None),
        P(),
    )
    return jax.shard_map(
        per_device,
        mesh=mesh,
        in_specs=placed,
        out_specs=(P("grp", None, "blk", None), P("grp", None, "blk", None)),
        check_vma=False,
    )
```

```python
import jax
import jax.numpy as jnp
import numpy as np
from jax import lax
from jax.experimental import pallas as pl
from jax.experimental.pallas import tpu as pltpu
from jax.sharding import PartitionSpec as P

MESH = pl.DeviceIdType.MESH
F32 = jnp.float32

lattice_vel = [
    (0, 0, 0), (1, 0, 0), (-1, 0, 0), (0, 1, 0), (0, -1, 0), (0, 0, 1), (0, 0, -1),
    (1, 1, 0), (-1, -1, 0), (1, -1, 0), (-1, 1, 0), (1, 0, 1), (-1, 0, -1),
    (1, 0, -1), (-1, 0, 1), (0, 1, 1), (0, -1, -1), (0, 1, -1), (0, -1, 1),
]
tau_fine = 0.6
tau_coarse = 0.55
rescale = 2.0 * tau_coarse / tau_fine
RIGHT = [i for i in range(19) if lattice_vel[i][0] == 1]
LEFT = [i for i in range(19) if lattice_vel[i][0] == -1]
STAY = [i for i in range(19) if lattice_vel[i][0] == 0]
X = 16
C = 8
ROW = 12
PAD = 8
HALVES = (0, 128)


def relaxed(f, keep_even, keep_odd, a):
    even = [None] * 19
    odd = [None] * 19
    for i in range(1, 19, 2):
        even[i] = f[i] + f[i + 1]
        odd[i] = f[i] - f[i + 1]
    rho = f[0]
    for i in range(1, 19, 2):
        rho = rho + even[i]
    j = []
    for axis in range(3):
        total = None
        for i in range(1, 19, 2):
            c = lattice_vel[i][axis]
            if c:
                term = odd[i]
                if total is None:
                    total = term if c > 0 else -term
                else:
                    total = total + term if c > 0 else total - term
        j.append(total)
    inverse = 1.0 / rho
    q = a * inverse
    jj = j[0] * j[0] + j[1] * j[1] + j[2] * j[2]
    base = a * rho - (1.5 * q) * jj
    out = [None] * 19
    out[0] = 2.0 * keep_even * f[0] + (1.0 / 3.0) * base
    axis_base = (1.0 / 18.0) * base
    edge_base = (1.0 / 36.0) * base
    axis_q = (4.5 / 18.0) * q
    edge_q = (4.5 / 36.0) * q
    axis_a = (3.0 / 18.0) * a
    edge_a = (3.0 / 36.0) * a
    for i in range(1, 19, 2):
        cj = None
        for axis in range(3):
            c = lattice_vel[i][axis]
            if c:
                if cj is None:
                    cj = j[axis] if c > 0 else -j[axis]
                else:
                    cj = cj + j[axis] if c > 0 else cj - j[axis]
        if i < 7:
            e = axis_base + axis_q * (cj * cj) + keep_even * even[i]
            o = axis_a * cj + keep_odd * odd[i]
        else:
            e = edge_base + edge_q * (cj * cj) + keep_even * even[i]
            o = edge_a * cj + keep_odd * odd[i]
        out[i] = e + o
        out[i + 1] = e - o
    return out


def collide(f, solid, tau):
    a = (1.0 - solid) * (1.0 / tau)
    keep_even = 0.5 * (1.0 - a)
    return relaxed(f, keep_even, keep_even - solid, a)


def lane_shift(low, high, cy, cz, lane):
    if cy == 0 and cz == 0:
        return low, high
    shift = 16 * cy + cz
    parts = []
    for v in (low, high):
        moved = pltpu.roll(v, shift % 128, 1)
        if cz:
            wrapped = pltpu.roll(v, (shift - 16 * cz) % 128, 1)
            z = lane % 16
            moved = jnp.where(z == (0 if cz > 0 else 15), wrapped, moved)
        parts.append(moved)
    if cy == 0:
        return parts[0], parts[1]
    crossing = lane < 16 if cy > 0 else lane >= 112
    return jnp.where(crossing, parts[1], parts[0]), jnp.where(crossing, parts[0], parts[1])


def lanes(rows):
    return lax.broadcasted_iota(jnp.int32, (rows, 128), 1)


def streamed(source, row, rows):
    lane = lanes(rows)
    low, high = [], []
    for i in range(19):
        cx, cy, cz = lattice_vel[i]
        start = row - cx
        a = source[i, start : start + rows, 0:128]
        b = source[i, start : start + rows, 128:256]
        a, b = lane_shift(a, b, cy, cz, lane)
        low.append(a)
        high.append(b)
    return low, high


def kernel(
    groups, blocks, slot_hbm, fine_hbm, solid_hbm, coarse_hbm, csolid_hbm,
    fine_view, solid_view, coarse_view, csolid_view, moved, settled,
    fine, solid, coarse, csolid, first, second, edge, boxes, inner, outer_r, outer_l,
    from_left, from_right, sol_left, sol_right, cfrom_left, cfrom_right, csol_left, csol_right,
    slot_ref, load_sem, ready, lefts, peers_in, halo_send, halo_recv, box_send, box_recv,
):
    g = lax.axis_index("grp")
    b = lax.axis_index("blk")
    right = (g, lax.rem(b + 1, blocks))
    left = (g, lax.rem(b + blocks - 1, blocks))
    half = groups // 2
    place = jnp.where(lax.rem(g, 2) == 1, g // 2, half + lax.rem(g // 2 + half - 1, half))
    peers = []
    for k in range(groups - 1):
        k = k + (place <= k).astype(jnp.int32)
        peers.append((jnp.where(k < half, 2 * k + 1, lax.rem(2 * (k - half) + 2, groups)), b))

    late = lax.rem(b, ROW) == ROW - 1
    follows = lax.rem(b, ROW) == 0

    barrier = pltpu.get_barrier_semaphore()
    pl.semaphore_signal(barrier, inc=1, device_id=left, device_id_type=MESH)

    @pl.when(jnp.logical_not(late))
    def _():
        for device in peers:
            pl.semaphore_signal(barrier, inc=1, device_id=device, device_id_type=MESH)

    loads = [
        pltpu.make_async_copy(solid_hbm.at[0], solid.at[PAD : PAD + X], load_sem.at[0]),
        pltpu.make_async_copy(fine_hbm.at[0], fine, load_sem.at[1]),
        pltpu.make_async_copy(csolid_hbm.at[0], csolid.at[PAD : PAD + C], load_sem.at[2]),
        pltpu.make_async_copy(coarse_hbm.at[0], coarse.at[:, PAD : PAD + C], load_sem.at[3]),
        pltpu.make_async_copy(slot_hbm, slot_ref, load_sem.at[4]),
    ]

    def halo(k, source, target, device):
        return pltpu.make_async_remote_copy(
            source, target, halo_send.at[k], halo_recv.at[k], device, MESH)

    halos_r = [
        halo(0, solid_view.at[1, :, 4:8], sol_left, right),
        halo(1, fine_view.at[:, 1, :, 4:8], from_left, right),
        halo(2, coarse_view.at[:, :, C - 1 : C], cfrom_left, right),
        halo(3, csolid_view.at[:, C - 1 : C], csol_left, right),
    ]
    halos_l = [
        halo(4, solid_view.at[0, :, 0:4], sol_right, left),
        halo(5, fine_view.at[:, 0, :, 0:4], from_right, left),
        halo(6, coarse_view.at[:, :, 0:1], cfrom_right, left),
        halo(7, csolid_view.at[:, 0:1], csol_right, left),
    ]
    pl.semaphore_wait(barrier, jnp.where(late, 1, groups))
    for copy in halos_r[:2]:
        copy.start()
    pl.semaphore_signal(ready, inc=1, device_id=right, device_id_type=MESH)
    for load in loads:
        load.start()

    def first_collision(f, s, start, rows, span):
        f = collide(f, s, tau_fine)
        for i in range(19):
            first[i, start : start + rows, span] = f[i]

    row = lax.broadcasted_iota(jnp.int32, (256, 128), 0)
    column = lax.broadcasted_iota(jnp.int32, (256, 128), 1)
    hit = (row // 32 == column // 16) & ((row % 16) // 2 == column % 8)
    boxes[...] = jnp.where(hit, 0.125, 0.0).astype(jnp.bfloat16)

    def second_collision(start, rows):
        low, high = streamed(first, start, rows)
        for f, h in ((low, 0), (high, 128)):
            span = slice(h, h + 128)
            f = collide(f, solid[start : start + rows, span], tau_fine)
            for i in range(19):
                second[i, start : start + rows, span] = f[i]

    def box_means(pair_sums):
        rest, parts = pair_sums, []
        for _ in range(3):
            piece = rest.astype(jnp.bfloat16).astype(F32)
            parts.append(piece)
            rest = rest - piece
        stacked = jnp.concatenate(parts, axis=0).astype(jnp.bfloat16)
        product = jnp.dot(stacked, boxes[...], preferred_element_type=F32)
        n = pair_sums.shape[0]
        return product[:n] + product[n : 2 * n] + product[2 * n :]

    def rescaled(means, rows):
        a = jnp.full((rows, 128), 1.0 - rescale, F32)
        keep = jnp.full((rows, 128), 0.5 * rescale, F32)
        return relaxed([means[rows * i : rows * i + rows] for i in range(19)], keep, keep, a)

    def near(rows):
        return lanes(rows) % 16 < 8

    def messages(which, buffer):
        return [
            pltpu.make_async_remote_copy(
                buffer.at[g], buffer.at[g], box_send.at[which, d], box_recv.at[which, g],
                peer, MESH)
            for d, peer in enumerate(peers)
        ]

    sends = [messages(0, inner), messages(1, outer_r), messages(2, outer_l)]

    def deliver(which):
        for send in sends[which]:
            send.start()

    def collect(which, buffer):
        for d, peer in enumerate(peers):
            pltpu.make_async_remote_copy(
                buffer.at[peer[0]], buffer.at[peer[0]], box_send.at[which, d],
                box_recv.at[which, peer[0]], peer, MESH).wait_recv()

    loads[0].wait()
    loads[1].wait()
    for t in range(X // 8):
        for h in HALVES:
            span = slice(h, h + 128)
            first_collision(
                [fine[i, 8 * t : 8 * t + 8, span] for i in range(19)],
                solid[PAD + 8 * t : PAD + 8 * t + 8, span], PAD + 8 * t, 8, span)
    for t in range(X // 8):
        second_collision(PAD + 8 * t, 8)
    for t in range(X // 8):
        low, high = streamed(second, PAD + 8 * t, 8)
        for i in range(19):
            moved[0, X * i + 8 * t : X * i + 8 * t + 8, :] = low[i]
            moved[1, X * i + 8 * t : X * i + 8 * t + 8, :] = high[i]
    sums = [
        moved[k, pl.ds(0, 152, stride=2), :] + moved[k, pl.ds(1, 152, stride=2), :]
        for k in range(2)
    ]
    f = rescaled(box_means(jnp.concatenate(sums, axis=1)), 8)
    for k in range(10):
        inner[g, k] = jnp.where(near(8), f[2 * k], f[min(2 * k + 1, 18)])

    @pl.when(jnp.logical_not(late))
    def _():
        deliver(0)

    for copy in halos_r[2:]:
        copy.start()

    pl.semaphore_wait(ready, 1)
    for copy in halos_l:
        copy.start()

    @pl.when(follows)
    def _():
        for device in peers:
            pl.semaphore_signal(lefts, inc=1, device_id=device, device_id_type=MESH)

    def beyond(halo, halo_solid, start):
        for k, h in enumerate(HALVES):
            span = slice(h, h + 128)
            s = halo_solid[k, :, 0, :]
            solid[start : start + 4, span] = s
            first_collision([halo[i, k, :, 0, :] for i in range(19)], s, start, 4, span)

    def outer_planes(side, outer):
        if side:
            low, high = streamed(second, PAD + X - 2, 4)
        else:
            low, high = streamed(second, PAD - 2, 4)
        for k, values in enumerate((low, high)):
            for i in range(19):
                edge[side, k, 4 * i : 4 * i + 4, :] = values[i]
                if side:
                    moved[k, X * i + X - 2 : X * i + X, :] = values[i][0:2]
                else:
                    moved[k, X * i : X * i + 2, :] = values[i][2:4]
        sums = [
            edge[side, k, pl.ds(0, 40, stride=2), :] + edge[side, k, pl.ds(1, 40, stride=2), :]
            for k in range(2)
        ]
        f = rescaled(box_means(jnp.concatenate(sums, axis=1)), 2)
        for k in range(10):
            outer[g, 2 * k : 2 * k + 2, :] = jnp.where(near(2), f[2 * k], f[min(2 * k + 1, 18)])

    halos_l[0].wait_recv()
    halos_l[1].wait_recv()
    beyond(from_right, sol_right, PAD + X)
    second_collision(PAD + X - 1, 4)
    outer_planes(1, outer_r)

    @pl.when(jnp.logical_not(late))
    def _():
        deliver(1)

    @pl.when(follows)
    def _():
        pl.semaphore_wait(lefts, groups - 1)
        pl.semaphore_signal(peers_in, inc=1, device_id=left, device_id_type=MESH)

    halos_r[0].wait_recv()
    halos_r[1].wait_recv()
    beyond(from_left, sol_left, PAD - 4)
    second_collision(PAD - 3, 4)
    outer_planes(0, outer_l)

    @pl.when(late)
    def _():
        pl.semaphore_wait(peers_in, 1)
        deliver(0)
        deliver(1)

    deliver(2)

    loads[4].wait()
    sources, present = [], []
    for q in range(4):
        source = jnp.int32(0)
        found = jnp.int32(0)
        for k in range(groups):
            match = (slot_ref[k] == 4 * g + q).astype(jnp.int32)
            source = jnp.maximum(source, k * match)
            found = jnp.maximum(found, match)
        sources.append(source)
        present.append(found)

    def pasted(half, rows, tile, start):
        span = slice(128 * half, 128 * half + 128)
        one, two = sources[2 * half], sources[2 * half + 1]
        close = near(rows)
        put = jnp.where(
            close,
            jnp.full((rows, 128), present[2 * half], jnp.int32),
            jnp.full((rows, 128), present[2 * half + 1], jnp.int32),
        ) > 0
        f = []
        for k in range(10):
            tile_one, tile_two = tile(one, k), tile(two, k)
            i = 2 * k
            value = jnp.where(close, tile_one, pltpu.roll(tile_two, 8, 1))
            f.append(jnp.where(put, value, coarse[i, start : start + rows, span]))
            if i + 1 < 19:
                value = jnp.where(close, pltpu.roll(tile_one, 120, 1), tile_two)
                f.append(jnp.where(put, value, coarse[i + 1, start : start + rows, span]))
        return collide(f, csolid[start : start + rows, span], tau_coarse), span

    def cbeyond(halo, halo_solid, start):
        for k, h in enumerate(HALVES):
            span = slice(h, h + 128)
            csolid[start : start + 1, span] = halo_solid[k, :, 0, :]
            for i in range(19):
                coarse[i, start : start + 1, span] = halo[i, k, :, 0, :]

    loads[2].wait()
    loads[3].wait()
    halos_l[2].wait_recv()
    halos_l[3].wait_recv()
    cbeyond(cfrom_right, csol_right, PAD + C)
    collect(0, inner)
    for half in range(2):
        f, span = pasted(half, C, lambda source, k: inner[source, k], PAD)
        for i in range(19):
            settled[i, PAD : PAD + C, span] = f[i]

    collect(1, outer_r)
    for half in range(2):
        f, span = pasted(
            half, 2, lambda source, k: outer_r[source, 2 * k : 2 * k + 2, :], PAD + C - 1)
        for i in range(19):
            settled[i, PAD + C - 1 : PAD + C + 1, span] = f[i]

    halos_r[2].wait_recv()
    halos_r[3].wait_recv()
    cbeyond(cfrom_left, csol_left, PAD - 1)
    collect(2, outer_l)
    for half in range(2):
        f, span = pasted(
            half, 2, lambda source, k: outer_l[source, 2 * k : 2 * k + 2, :], PAD - 1)
        for i in range(19):
            settled[i, PAD - 1 : PAD + 1, span] = f[i]

    for copy in halos_r + halos_l + sends[0] + sends[1] + sends[2]:
        copy.wait_send()


def finish(moved, settled, fine_out, coarse_out, cmoved, store_sem):
    stores = [
        pltpu.make_async_copy(moved.at[k], fine_out.at[0, :, :, h : h + 128], store_sem.at[k])
        for k, h in enumerate(HALVES)
    ]
    for store in stores:
        store.start()
    low, high = streamed(settled, PAD, C)
    for i in range(19):
        cmoved[i, :, 0:128] = low[i]
        cmoved[i, :, 128:256] = high[i]
    stores.append(pltpu.make_async_copy(cmoved, coarse_out.at[0], store_sem.at[2]))
    stores[2].start()
    for store in stores:
        store.wait()


def solution(mesh):
    groups, blocks = mesh.shape["grp"], mesh.shape["blk"]
    vmem = pl.BlockSpec(memory_space=pltpu.VMEM)
    hbm = pl.BlockSpec(memory_space=pltpu.HBM)

    def planes(x, *leading):
        n = len(leading)
        order = tuple(range(n)) + (n + 1, n, n + 2)
        x = x.reshape(leading + (8, 2, 128)).transpose(order)
        return x.reshape(leading + (2, 8, 1, 128))

    def per_device(fine_pops, fine_solid, coarse_pops, coarse_solid, coarse_slot):
        body = lambda *refs: kernel(groups, blocks, *refs)
        moved, settled = pl.pallas_call(
            body,
            out_shape=(
                jax.ShapeDtypeStruct((2, 19 * X, 128), F32),
                jax.ShapeDtypeStruct((19, C + 2 * PAD, 256), F32),
            ),
            in_specs=[hbm] * 9,
            out_specs=(vmem, vmem),
            scratch_shapes=[
                pltpu.VMEM((19, X, 256), F32),
                pltpu.VMEM((X + 2 * PAD, 256), F32),
                pltpu.VMEM((19, C + 2 * PAD, 256), F32),
                pltpu.VMEM((C + 2 * PAD, 256), F32),
                pltpu.VMEM((19, X + 2 * PAD, 256), F32),
                pltpu.VMEM((19, X + 2 * PAD, 256), F32),
                pltpu.VMEM((2, 2, 80, 128), F32),
                pltpu.VMEM((256, 128), jnp.bfloat16),
                pltpu.VMEM((groups, 10, 8, 128), F32),
                pltpu.VMEM((groups, 24, 128), F32),
                pltpu.VMEM((groups, 24, 128), F32),
            ]
            + [pltpu.VMEM((19, 2, 4, 1, 128), F32)] * 2
            + [pltpu.VMEM((2, 4, 1, 128), F32)] * 2
            + [pltpu.VMEM((19, 2, 1, 1, 128), F32)] * 2
            + [pltpu.VMEM((2, 1, 1, 128), F32)] * 2
            + [
                pltpu.SMEM((groups,), jnp.int32),
                pltpu.SemaphoreType.DMA((5,)),
                pltpu.SemaphoreType.REGULAR,
                pltpu.SemaphoreType.REGULAR,
                pltpu.SemaphoreType.REGULAR,
                pltpu.SemaphoreType.DMA((8,)),
                pltpu.SemaphoreType.DMA((8,)),
                pltpu.SemaphoreType.DMA((3, groups)),
                pltpu.SemaphoreType.DMA((3, groups)),
            ],
            compiler_params=pltpu.CompilerParams(
                collective_id=0, has_side_effects=True, vmem_limit_bytes=16 << 20),
        )(*[
            pltpu.with_memory_space_constraint(x, pltpu.HBM)
            for x in (
                coarse_slot, fine_pops, fine_solid, coarse_pops, coarse_solid,
                planes(fine_pops, 19, 2), planes(fine_solid, 2),
                planes(coarse_pops, 19), planes(coarse_solid),
            )
        ])
        return pl.pallas_call(
            finish,
            out_shape=(
                jax.ShapeDtypeStruct(fine_pops.shape, F32),
                jax.ShapeDtypeStruct(coarse_pops.shape, F32),
            ),
            in_specs=[vmem, vmem],
            out_specs=(hbm, hbm),
            scratch_shapes=[pltpu.VMEM((19, C, 256), F32), pltpu.SemaphoreType.DMA((3,))],
            compiler_params=pltpu.CompilerParams(vmem_limit_bytes=4 << 20),
        )(moved.reshape(2, 19, X, 128), settled)

    placed = (
        P("grp", None, "blk", None),
        P("grp", "blk", None),
        P("grp", None, "blk", None),
        P("grp", "blk", None),
        P(),
    )
    return jax.shard_map(
        per_device,
        mesh=mesh,
        in_specs=placed,
        out_specs=(P("grp", None, "blk", None), P("grp", None, "blk", None)),
        check_vma=False,
    )
```

```python
import jax
import jax.numpy as jnp
import numpy as np
from jax import lax
from jax.experimental import pallas as pl
from jax.experimental.pallas import tpu as pltpu
from jax.sharding import PartitionSpec as P

MESH = pl.DeviceIdType.MESH
F32 = jnp.float32

lattice_vel = [
    (0, 0, 0), (1, 0, 0), (-1, 0, 0), (0, 1, 0), (0, -1, 0), (0, 0, 1), (0, 0, -1),
    (1, 1, 0), (-1, -1, 0), (1, -1, 0), (-1, 1, 0), (1, 0, 1), (-1, 0, -1),
    (1, 0, -1), (-1, 0, 1), (0, 1, 1), (0, -1, -1), (0, 1, -1), (0, -1, 1),
]
tau_fine = 0.6
tau_coarse = 0.55
rescale = 2.0 * tau_coarse / tau_fine
RIGHT = [i for i in range(19) if lattice_vel[i][0] == 1]
LEFT = [i for i in range(19) if lattice_vel[i][0] == -1]
STAY = [i for i in range(19) if lattice_vel[i][0] == 0]
X = 16
C = 8
ROW = 12
PAD = 8
HALVES = (0, 128)


def total(terms):
    while len(terms) > 1:
        terms = [a + b for a, b in zip(terms[::2], terms[1::2])] + terms[len(terms) // 2 * 2 :]
    return terms[0]


def relaxed(f, keep_even, keep_odd, a):
    even = [None] * 19
    odd = [None] * 19
    for i in range(1, 19, 2):
        even[i] = f[i] + f[i + 1]
        odd[i] = f[i] - f[i + 1]
    rho = total([f[0]] + [even[i] for i in range(1, 19, 2)])
    j = []
    for axis in range(3):
        plus = [odd[i] for i in range(1, 19, 2) if lattice_vel[i][axis] > 0]
        minus = [odd[i] for i in range(1, 19, 2) if lattice_vel[i][axis] < 0]
        j.append(total(plus) - total(minus) if minus else total(plus))
    inverse = 1.0 / rho
    q = a * inverse
    jj = j[0] * j[0] + j[1] * j[1] + j[2] * j[2]
    base = a * rho - (1.5 * q) * jj
    out = [None] * 19
    out[0] = 2.0 * keep_even * f[0] + (1.0 / 3.0) * base
    axis_base = (1.0 / 18.0) * base
    edge_base = (1.0 / 36.0) * base
    axis_q = (4.5 / 18.0) * q
    edge_q = (4.5 / 36.0) * q
    axis_a = (3.0 / 18.0) * a
    edge_a = (3.0 / 36.0) * a
    for i in range(1, 19, 2):
        cj = None
        for axis in range(3):
            c = lattice_vel[i][axis]
            if c:
                if cj is None:
                    cj = j[axis] if c > 0 else -j[axis]
                else:
                    cj = cj + j[axis] if c > 0 else cj - j[axis]
        if i < 7:
            e = axis_base + axis_q * (cj * cj) + keep_even * even[i]
            o = axis_a * cj + keep_odd * odd[i]
        else:
            e = edge_base + edge_q * (cj * cj) + keep_even * even[i]
            o = edge_a * cj + keep_odd * odd[i]
        out[i] = e + o
        out[i + 1] = e - o
    return out


def collide(f, solid, tau):
    a = (1.0 - solid) * (1.0 / tau)
    keep_even = 0.5 * (1.0 - a)
    return relaxed(f, keep_even, keep_even - solid, a)


def lane_shift(low, high, cy, cz, lane):
    if cy == 0 and cz == 0:
        return low, high
    shift = 16 * cy + cz
    parts = []
    for v in (low, high):
        moved = pltpu.roll(v, shift % 128, 1)
        if cz:
            wrapped = pltpu.roll(v, (shift - 16 * cz) % 128, 1)
            z = lane % 16
            moved = jnp.where(z == (0 if cz > 0 else 15), wrapped, moved)
        parts.append(moved)
    if cy == 0:
        return parts[0], parts[1]
    crossing = lane < 16 if cy > 0 else lane >= 112
    return jnp.where(crossing, parts[1], parts[0]), jnp.where(crossing, parts[0], parts[1])


def lanes(rows):
    return lax.broadcasted_iota(jnp.int32, (rows, 128), 1)


def streamed(source, row, rows):
    lane = lanes(rows)
    low, high = [], []
    for i in range(19):
        cx, cy, cz = lattice_vel[i]
        start = row - cx
        a = source[i, start : start + rows, 0:128]
        b = source[i, start : start + rows, 128:256]
        a, b = lane_shift(a, b, cy, cz, lane)
        low.append(a)
        high.append(b)
    return low, high


def packed(source, row):
    lane = lanes(8)
    odd = lax.broadcasted_iota(jnp.int32, (8, 128), 0) % 2 == 1
    out = []
    for i in range(19):
        cx, cy, cz = lattice_vel[i]
        start = 16 * i + row - 2 * cx
        v = source[start : start + 8, :]
        if cy or cz:
            shift = 16 * cy + cz
            m = pltpu.roll(v, shift % 128, 1)
            if cz:
                wrapped = pltpu.roll(v, (shift - 16 * cz) % 128, 1)
                m = jnp.where(lane % 16 == (0 if cz > 0 else 15), wrapped, m)
            if cy:
                other = jnp.where(odd, pltpu.roll(m, 1, 0), pltpu.roll(m, 7, 0))
                m = jnp.where(lane < 16 if cy > 0 else lane >= 112, other, m)
            v = m
        out.append(v)
    return out


def kernel(
    groups, blocks, slot_hbm, fine_hbm, solid_hbm, coarse_hbm, csolid_hbm,
    fine_view, solid_view, coarse_view, csolid_view, moved, settled,
    fine, solid, coarse, csolid, first, second, edge, pfirst, psecond, psolid, pmoved, boxes, inner, outer_r, outer_l,
    from_left, from_right, sol_left, sol_right, cfrom_left, cfrom_right, csol_left, csol_right,
    slot_ref, load_sem, ready, lefts, peers_in, halo_send, halo_recv, box_send, box_recv,
):
    g = lax.axis_index("grp")
    b = lax.axis_index("blk")
    right = (g, lax.rem(b + 1, blocks))
    left = (g, lax.rem(b + blocks - 1, blocks))
    half = groups // 2
    place = jnp.where(lax.rem(g, 2) == 1, g // 2, half + lax.rem(g // 2 + half - 1, half))
    peers = []
    for k in range(groups - 1):
        k = k + (place <= k).astype(jnp.int32)
        peers.append((jnp.where(k < half, 2 * k + 1, lax.rem(2 * (k - half) + 2, groups)), b))

    late = lax.rem(b, ROW) == ROW - 1
    follows = lax.rem(b, ROW) == 0

    barrier = pltpu.get_barrier_semaphore()
    pl.semaphore_signal(barrier, inc=1, device_id=left, device_id_type=MESH)

    @pl.when(jnp.logical_not(late))
    def _():
        for device in peers:
            pl.semaphore_signal(barrier, inc=1, device_id=device, device_id_type=MESH)

    loads = [
        pltpu.make_async_copy(solid_hbm.at[0], solid.at[PAD : PAD + X], load_sem.at[0]),
        pltpu.make_async_copy(fine_hbm.at[0], fine, load_sem.at[1]),
        pltpu.make_async_copy(csolid_hbm.at[0], csolid.at[PAD : PAD + C], load_sem.at[2]),
        pltpu.make_async_copy(coarse_hbm.at[0], coarse.at[:, PAD : PAD + C], load_sem.at[3]),
        pltpu.make_async_copy(slot_hbm, slot_ref, load_sem.at[4]),
    ]

    def halo(k, source, target, device):
        return pltpu.make_async_remote_copy(
            source, target, halo_send.at[k], halo_recv.at[k], device, MESH)

    halos_r = [
        halo(0, solid_view.at[1, :, 4:8], sol_left, right),
        halo(1, fine_view.at[:, 1, :, 4:8], from_left, right),
        halo(2, coarse_view.at[:, :, C - 1 : C], cfrom_left, right),
        halo(3, csolid_view.at[:, C - 1 : C], csol_left, right),
    ]
    halos_l = [
        halo(4, solid_view.at[0, :, 0:4], sol_right, left),
        halo(5, fine_view.at[:, 0, :, 0:4], from_right, left),
        halo(6, coarse_view.at[:, :, 0:1], cfrom_right, left),
        halo(7, csolid_view.at[:, 0:1], csol_right, left),
    ]
    pl.semaphore_wait(barrier, jnp.where(late, 1, groups))
    for copy in halos_r[:2]:
        copy.start()
    pl.semaphore_signal(ready, inc=1, device_id=right, device_id_type=MESH)
    for load in loads:
        load.start()

    def first_collision(f, s, start, rows, span):
        f = collide(f, s, tau_fine)
        for i in range(19):
            first[i, start : start + rows, span] = f[i]

    row = lax.broadcasted_iota(jnp.int32, (256, 128), 0)
    column = lax.broadcasted_iota(jnp.int32, (256, 128), 1)
    hit = (row // 32 == column // 16) & ((row % 16) // 2 == column % 8)
    boxes[...] = jnp.where(hit, 0.125, 0.0).astype(jnp.bfloat16)

    def second_collision(start, rows):
        low, high = streamed(first, start, rows)
        for f, h in ((low, 0), (high, 128)):
            span = slice(h, h + 128)
            f = collide(f, solid[start : start + rows, span], tau_fine)
            for i in range(19):
                second[i, start : start + rows, span] = f[i]

    def box_means(pair_sums):
        rest, parts = pair_sums, []
        for _ in range(3):
            piece = rest.astype(jnp.bfloat16).astype(F32)
            parts.append(piece)
            rest = rest - piece
        stacked = jnp.concatenate(parts, axis=0).astype(jnp.bfloat16)
        product = jnp.dot(stacked, boxes[...], preferred_element_type=F32)
        n = pair_sums.shape[0]
        return product[:n] + product[n : 2 * n] + product[2 * n :]

    def rescaled(means, rows):
        a = jnp.full((rows, 128), 1.0 - rescale, F32)
        keep = jnp.full((rows, 128), 0.5 * rescale, F32)
        return relaxed([means[rows * i : rows * i + rows] for i in range(19)], keep, keep, a)

    def near(rows):
        return lanes(rows) % 16 < 8

    def messages(which, buffer):
        return [
            pltpu.make_async_remote_copy(
                buffer.at[g], buffer.at[g], box_send.at[which, d], box_recv.at[which, g],
                peer, MESH)
            for d, peer in enumerate(peers)
        ]

    sends = [messages(0, inner), messages(1, outer_r), messages(2, outer_l)]

    def deliver(which):
        for send in sends[which]:
            send.start()

    def collect(which, buffer):
        for d, peer in enumerate(peers):
            pltpu.make_async_remote_copy(
                buffer.at[peer[0]], buffer.at[peer[0]], box_send.at[which, d],
                box_recv.at[which, peer[0]], peer, MESH).wait_recv()

    loads[0].wait()
    loads[1].wait()
    for t in range(X // 8):
        for h in HALVES:
            span = slice(h, h + 128)
            first_collision(
                [fine[i, 8 * t : 8 * t + 8, span] for i in range(19)],
                solid[PAD + 8 * t : PAD + 8 * t + 8, span], PAD + 8 * t, 8, span)
    for k, h in enumerate(HALVES):
        span = slice(h, h + 128)
        psolid[pl.ds(8 + k, 4, stride=2), :] = solid[PAD : PAD + 4, span]
        for i in range(19):
            pfirst[pl.ds(16 * i + 8 + k, 4, stride=2), :] = first[i, PAD : PAD + 4, span]
    for t in range(X // 8):
        second_collision(PAD + 8 * t, 8)
    for k, h in enumerate(HALVES):
        for i in range(19):
            psecond[pl.ds(16 * i + 10 + k, 2, stride=2), :] = second[
                i, PAD + 1 : PAD + 3, h : h + 128]
    for t in range(X // 8):
        low, high = streamed(second, PAD + 8 * t, 8)
        for i in range(19):
            moved[0, X * i + 8 * t : X * i + 8 * t + 8, :] = low[i]
            moved[1, X * i + 8 * t : X * i + 8 * t + 8, :] = high[i]
    sums = [
        moved[k, pl.ds(0, 152, stride=2), :] + moved[k, pl.ds(1, 152, stride=2), :]
        for k in range(2)
    ]
    f = rescaled(box_means(jnp.concatenate(sums, axis=1)), 8)
    for k in range(10):
        inner[g, k] = jnp.where(near(8), f[2 * k], f[min(2 * k + 1, 18)])

    @pl.when(jnp.logical_not(late))
    def _():
        deliver(0)

    for copy in halos_r[2:]:
        copy.start()

    pl.semaphore_wait(ready, 1)
    for copy in halos_l:
        copy.start()

    @pl.when(follows)
    def _():
        for device in peers:
            pl.semaphore_signal(lefts, inc=1, device_id=device, device_id_type=MESH)

    def beyond(halo, halo_solid, start):
        for k, h in enumerate(HALVES):
            span = slice(h, h + 128)
            s = halo_solid[k, :, 0, :]
            solid[start : start + 4, span] = s
            first_collision([halo[i, k, :, 0, :] for i in range(19)], s, start, 4, span)

    def restricted(sums, outer):
        f = rescaled(box_means(jnp.concatenate(sums, axis=1)), 2)
        for k in range(10):
            outer[g, 2 * k : 2 * k + 2, :] = jnp.where(near(2), f[2 * k], f[min(2 * k + 1, 18)])

    halos_l[0].wait_recv()
    halos_l[1].wait_recv()
    beyond(from_right, sol_right, PAD + X)
    second_collision(PAD + X - 1, 4)
    low, high = streamed(second, PAD + X - 2, 4)
    for k, values in enumerate((low, high)):
        for i in range(19):
            edge[k, 4 * i : 4 * i + 4, :] = values[i]
            moved[k, X * i + X - 2 : X * i + X, :] = values[i][0:2]
    restricted(
        [edge[k, pl.ds(0, 40, stride=2), :] + edge[k, pl.ds(1, 40, stride=2), :] for k in range(2)],
        outer_r)

    @pl.when(jnp.logical_not(late))
    def _():
        deliver(1)

    @pl.when(follows)
    def _():
        pl.semaphore_wait(lefts, groups - 1)
        pl.semaphore_signal(peers_in, inc=1, device_id=left, device_id_type=MESH)

    halos_r[0].wait_recv()
    halos_r[1].wait_recv()
    s = sol_left[...].reshape(8, 128)
    f = collide([from_left[i].reshape(8, 128) for i in range(19)], s, tau_fine)
    for k in range(2):
        psolid[pl.ds(k, 4, stride=2), :] = s[4 * k : 4 * k + 4]
        for i in range(19):
            pfirst[pl.ds(16 * i + k, 4, stride=2), :] = f[i][4 * k : 4 * k + 4]
    f = collide(packed(pfirst, 2), psolid[2:10, :], tau_fine)
    for i in range(19):
        psecond[16 * i + 2 : 16 * i + 10, :] = f[i]
    f = packed(psecond, 4)
    for i in range(19):
        pmoved[8 * i : 8 * i + 8, :] = f[i]
    restricted(
        [pmoved[pl.ds(k, 40, stride=4), :] + pmoved[pl.ds(k + 2, 40, stride=4), :]
         for k in range(2)],
        outer_l)

    @pl.when(late)
    def _():
        pl.semaphore_wait(peers_in, 1)
        deliver(0)
        deliver(1)

    deliver(2)
    for k in range(2):
        for i in range(19):
            moved[k, X * i : X * i + 2, :] = pmoved[pl.ds(8 * i + 4 + k, 2, stride=2), :]

    loads[4].wait()
    sources, present = [], []
    for q in range(4):
        source = jnp.int32(0)
        found = jnp.int32(0)
        for k in range(groups):
            match = (slot_ref[k] == 4 * g + q).astype(jnp.int32)
            source = jnp.maximum(source, k * match)
            found = jnp.maximum(found, match)
        sources.append(source)
        present.append(found)

    def pasted(half, rows, tile, start):
        span = slice(128 * half, 128 * half + 128)
        one, two = sources[2 * half], sources[2 * half + 1]
        close = near(rows)
        put = jnp.where(
            close,
            jnp.full((rows, 128), present[2 * half], jnp.int32),
            jnp.full((rows, 128), present[2 * half + 1], jnp.int32),
        ) > 0
        f = []
        for k in range(10):
            tile_one, tile_two = tile(one, k), tile(two, k)
            i = 2 * k
            value = jnp.where(close, tile_one, pltpu.roll(tile_two, 8, 1))
            f.append(jnp.where(put, value, coarse[i, start : start + rows, span]))
            if i + 1 < 19:
                value = jnp.where(close, pltpu.roll(tile_one, 120, 1), tile_two)
                f.append(jnp.where(put, value, coarse[i + 1, start : start + rows, span]))
        return collide(f, csolid[start : start + rows, span], tau_coarse), span

    def cbeyond(halo, halo_solid, start):
        for k, h in enumerate(HALVES):
            span = slice(h, h + 128)
            csolid[start : start + 1, span] = halo_solid[k, :, 0, :]
            for i in range(19):
                coarse[i, start : start + 1, span] = halo[i, k, :, 0, :]

    loads[2].wait()
    loads[3].wait()
    halos_l[2].wait_recv()
    halos_l[3].wait_recv()
    cbeyond(cfrom_right, csol_right, PAD + C)
    collect(0, inner)
    for half in range(2):
        f, span = pasted(half, C, lambda source, k: inner[source, k], PAD)
        for i in range(19):
            settled[i, PAD : PAD + C, span] = f[i]

    collect(1, outer_r)
    for half in range(2):
        f, span = pasted(
            half, 2, lambda source, k: outer_r[source, 2 * k : 2 * k + 2, :], PAD + C - 1)
        for i in range(19):
            settled[i, PAD + C - 1 : PAD + C + 1, span] = f[i]

    halos_r[2].wait_recv()
    halos_r[3].wait_recv()
    cbeyond(cfrom_left, csol_left, PAD - 1)
    for copy in halos_r + halos_l + sends[0] + sends[1]:
        copy.wait_send()
    collect(2, outer_l)
    for half in range(2):
        f, span = pasted(
            half, 2, lambda source, k: outer_l[source, 2 * k : 2 * k + 2, :], PAD - 1)
        for i in range(19):
            settled[i, PAD - 1 : PAD + 1, span] = f[i]

    for copy in sends[2]:
        copy.wait_send()


def finish(moved, settled, fine_out, coarse_out, cmoved, store_sem):
    stores = [
        pltpu.make_async_copy(moved.at[k], fine_out.at[0, :, :, h : h + 128], store_sem.at[k])
        for k, h in enumerate(HALVES)
    ]
    for store in stores:
        store.start()
    low, high = streamed(settled, PAD, C)
    for i in range(19):
        cmoved[i, :, 0:128] = low[i]
        cmoved[i, :, 128:256] = high[i]
    stores.append(pltpu.make_async_copy(cmoved, coarse_out.at[0], store_sem.at[2]))
    stores[2].start()
    for store in stores:
        store.wait()


def solution(mesh):
    groups, blocks = mesh.shape["grp"], mesh.shape["blk"]
    vmem = pl.BlockSpec(memory_space=pltpu.VMEM)
    hbm = pl.BlockSpec(memory_space=pltpu.HBM)

    def planes(x, *leading):
        n = len(leading)
        order = tuple(range(n)) + (n + 1, n, n + 2)
        x = x.reshape(leading + (8, 2, 128)).transpose(order)
        return x.reshape(leading + (2, 8, 1, 128))

    def per_device(fine_pops, fine_solid, coarse_pops, coarse_solid, coarse_slot):
        body = lambda *refs: kernel(groups, blocks, *refs)
        moved, settled = pl.pallas_call(
            body,
            out_shape=(
                jax.ShapeDtypeStruct((2, 19 * X, 128), F32),
                jax.ShapeDtypeStruct((19, C + 2 * PAD, 256), F32),
            ),
            in_specs=[hbm] * 9,
            out_specs=(vmem, vmem),
            scratch_shapes=[
                pltpu.VMEM((19, X, 256), F32),
                pltpu.VMEM((X + 2 * PAD, 256), F32),
                pltpu.VMEM((19, C + 2 * PAD, 256), F32),
                pltpu.VMEM((C + 2 * PAD, 256), F32),
                pltpu.VMEM((19, X + 2 * PAD, 256), F32),
                pltpu.VMEM((19, X + 2 * PAD, 256), F32),
                pltpu.VMEM((2, 80, 128), F32),
                pltpu.VMEM((19 * 16, 128), F32),
                pltpu.VMEM((19 * 16, 128), F32),
                pltpu.VMEM((16, 128), F32),
                pltpu.VMEM((160, 128), F32),
                pltpu.VMEM((256, 128), jnp.bfloat16),
                pltpu.VMEM((groups, 10, 8, 128), F32),
                pltpu.VMEM((groups, 24, 128), F32),
                pltpu.VMEM((groups, 24, 128), F32),
            ]
            + [pltpu.VMEM((19, 2, 4, 1, 128), F32)] * 2
            + [pltpu.VMEM((2, 4, 1, 128), F32)] * 2
            + [pltpu.VMEM((19, 2, 1, 1, 128), F32)] * 2
            + [pltpu.VMEM((2, 1, 1, 128), F32)] * 2
            + [
                pltpu.SMEM((groups,), jnp.int32),
                pltpu.SemaphoreType.DMA((5,)),
                pltpu.SemaphoreType.REGULAR,
                pltpu.SemaphoreType.REGULAR,
                pltpu.SemaphoreType.REGULAR,
                pltpu.SemaphoreType.DMA((8,)),
                pltpu.SemaphoreType.DMA((8,)),
                pltpu.SemaphoreType.DMA((3, groups)),
                pltpu.SemaphoreType.DMA((3, groups)),
            ],
            compiler_params=pltpu.CompilerParams(
                collective_id=0, has_side_effects=True, vmem_limit_bytes=16 << 20),
        )(*[
            pltpu.with_memory_space_constraint(x, pltpu.HBM)
            for x in (
                coarse_slot, fine_pops, fine_solid, coarse_pops, coarse_solid,
                planes(fine_pops, 19, 2), planes(fine_solid, 2),
                planes(coarse_pops, 19), planes(coarse_solid),
            )
        ])
        return pl.pallas_call(
            finish,
            out_shape=(
                jax.ShapeDtypeStruct(fine_pops.shape, F32),
                jax.ShapeDtypeStruct(coarse_pops.shape, F32),
            ),
            in_specs=[vmem, vmem],
            out_specs=(hbm, hbm),
            scratch_shapes=[pltpu.VMEM((19, C, 256), F32), pltpu.SemaphoreType.DMA((3,))],
            compiler_params=pltpu.CompilerParams(vmem_limit_bytes=4 << 20),
        )(moved.reshape(2, 19, X, 128), settled)

    placed = (
        P("grp", None, "blk", None),
        P("grp", "blk", None),
        P("grp", None, "blk", None),
        P("grp", "blk", None),
        P(),
    )
    return jax.shard_map(
        per_device,
        mesh=mesh,
        in_specs=placed,
        out_specs=(P("grp", None, "blk", None), P("grp", None, "blk", None)),
        check_vma=False,
    )
```

```python
import jax
import jax.numpy as jnp
import numpy as np
from jax import lax
from jax.experimental import pallas as pl
from jax.experimental.pallas import tpu as pltpu
from jax.sharding import PartitionSpec as P

MESH = pl.DeviceIdType.MESH
F32 = jnp.float32

lattice_vel = [
    (0, 0, 0), (1, 0, 0), (-1, 0, 0), (0, 1, 0), (0, -1, 0), (0, 0, 1), (0, 0, -1),
    (1, 1, 0), (-1, -1, 0), (1, -1, 0), (-1, 1, 0), (1, 0, 1), (-1, 0, -1),
    (1, 0, -1), (-1, 0, 1), (0, 1, 1), (0, -1, -1), (0, 1, -1), (0, -1, 1),
]
tau_fine = 0.6
tau_coarse = 0.55
rescale = 2.0 * tau_coarse / tau_fine
RIGHT = [i for i in range(19) if lattice_vel[i][0] == 1]
LEFT = [i for i in range(19) if lattice_vel[i][0] == -1]
STAY = [i for i in range(19) if lattice_vel[i][0] == 0]
X = 16
C = 8
ROW = 12
PAD = 8
HALVES = (0, 128)


def total(terms):
    while len(terms) > 1:
        terms = [a + b for a, b in zip(terms[::2], terms[1::2])] + terms[len(terms) // 2 * 2 :]
    return terms[0]


def relaxed(f, keep_even, keep_odd, a):
    even = [None] * 19
    odd = [None] * 19
    for i in range(1, 19, 2):
        even[i] = f[i] + f[i + 1]
        odd[i] = f[i] - f[i + 1]
    rho = total([f[0]] + [even[i] for i in range(1, 19, 2)])
    j = []
    for axis in range(3):
        plus = [odd[i] for i in range(1, 19, 2) if lattice_vel[i][axis] > 0]
        minus = [odd[i] for i in range(1, 19, 2) if lattice_vel[i][axis] < 0]
        j.append(total(plus) - total(minus) if minus else total(plus))
    inverse = 1.0 / rho
    q = a * inverse
    jj = j[0] * j[0] + j[1] * j[1] + j[2] * j[2]
    base = a * rho - (1.5 * q) * jj
    out = [None] * 19
    out[0] = 2.0 * keep_even * f[0] + (1.0 / 3.0) * base
    axis_base = (1.0 / 18.0) * base
    edge_base = (1.0 / 36.0) * base
    axis_q = (4.5 / 18.0) * q
    edge_q = (4.5 / 36.0) * q
    axis_a = (3.0 / 18.0) * a
    edge_a = (3.0 / 36.0) * a
    for i in range(1, 19, 2):
        cj = None
        for axis in range(3):
            c = lattice_vel[i][axis]
            if c:
                if cj is None:
                    cj = j[axis] if c > 0 else -j[axis]
                else:
                    cj = cj + j[axis] if c > 0 else cj - j[axis]
        if i < 7:
            e = axis_base + axis_q * (cj * cj) + keep_even * even[i]
            o = axis_a * cj + keep_odd * odd[i]
        else:
            e = edge_base + edge_q * (cj * cj) + keep_even * even[i]
            o = edge_a * cj + keep_odd * odd[i]
        out[i] = e + o
        out[i + 1] = e - o
    return out


def collide(f, solid, tau):
    a = (1.0 - solid) * (1.0 / tau)
    keep_even = 0.5 * (1.0 - a)
    return relaxed(f, keep_even, keep_even - solid, a)


def lane_shift(low, high, cy, cz, lane):
    if cy == 0 and cz == 0:
        return low, high
    shift = 16 * cy + cz
    parts = []
    for v in (low, high):
        moved = pltpu.roll(v, shift % 128, 1)
        if cz:
            wrapped = pltpu.roll(v, (shift - 16 * cz) % 128, 1)
            z = lane % 16
            moved = jnp.where(z == (0 if cz > 0 else 15), wrapped, moved)
        parts.append(moved)
    if cy == 0:
        return parts[0], parts[1]
    crossing = lane < 16 if cy > 0 else lane >= 112
    return jnp.where(crossing, parts[1], parts[0]), jnp.where(crossing, parts[0], parts[1])


def lanes(rows):
    return lax.broadcasted_iota(jnp.int32, (rows, 128), 1)


def streamed(source, row, rows):
    lane = lanes(rows)
    low, high = [], []
    for i in range(19):
        cx, cy, cz = lattice_vel[i]
        start = row - cx
        a = source[i, start : start + rows, 0:128]
        b = source[i, start : start + rows, 128:256]
        a, b = lane_shift(a, b, cy, cz, lane)
        low.append(a)
        high.append(b)
    return low, high


def packed(source, row):
    lane = lanes(8)
    odd = lax.broadcasted_iota(jnp.int32, (8, 128), 0) % 2 == 1
    out = []
    for i in range(19):
        cx, cy, cz = lattice_vel[i]
        start = 16 * i + row - 2 * cx
        v = source[start : start + 8, :]
        if cy or cz:
            shift = 16 * cy + cz
            m = pltpu.roll(v, shift % 128, 1)
            if cz:
                wrapped = pltpu.roll(v, (shift - 16 * cz) % 128, 1)
                m = jnp.where(lane % 16 == (0 if cz > 0 else 15), wrapped, m)
            if cy:
                other = jnp.where(odd, pltpu.roll(m, 1, 0), pltpu.roll(m, 7, 0))
                m = jnp.where(lane < 16 if cy > 0 else lane >= 112, other, m)
            v = m
        out.append(v)
    return out


def kernel(
    groups, blocks, slot_hbm, fine_hbm, solid_hbm, coarse_hbm, csolid_hbm,
    fine_view, solid_view, coarse_view, csolid_view, moved, settled,
    fine, solid, coarse, csolid, first, second, edge, pfirst, psecond, psolid, pmoved, means, boxes, inner, outer_r, outer_l,
    from_left, from_right, sol_left, sol_right, cfrom_left, cfrom_right, csol_left, csol_right,
    slot_ref, load_sem, ready, lefts, peers_in, halo_send, halo_recv, box_send, box_recv,
):
    g = lax.axis_index("grp")
    b = lax.axis_index("blk")
    right = (g, lax.rem(b + 1, blocks))
    left = (g, lax.rem(b + blocks - 1, blocks))
    half = groups // 2
    place = jnp.where(lax.rem(g, 2) == 1, g // 2, half + lax.rem(g // 2 + half - 1, half))
    peers = []
    for k in range(groups - 1):
        k = k + (place <= k).astype(jnp.int32)
        peers.append((jnp.where(k < half, 2 * k + 1, lax.rem(2 * (k - half) + 2, groups)), b))

    late = lax.rem(b, ROW) == ROW - 1
    follows = lax.rem(b, ROW) == 0

    barrier = pltpu.get_barrier_semaphore()
    pl.semaphore_signal(barrier, inc=1, device_id=left, device_id_type=MESH)

    @pl.when(jnp.logical_not(late))
    def _():
        for device in peers:
            pl.semaphore_signal(barrier, inc=1, device_id=device, device_id_type=MESH)

    loads = [
        pltpu.make_async_copy(solid_hbm.at[0], solid.at[PAD : PAD + X], load_sem.at[0]),
        pltpu.make_async_copy(fine_hbm.at[0], fine, load_sem.at[1]),
        pltpu.make_async_copy(csolid_hbm.at[0], csolid.at[PAD : PAD + C], load_sem.at[2]),
        pltpu.make_async_copy(coarse_hbm.at[0], coarse.at[:, PAD : PAD + C], load_sem.at[3]),
        pltpu.make_async_copy(slot_hbm, slot_ref, load_sem.at[4]),
    ]

    def halo(k, source, target, device):
        return pltpu.make_async_remote_copy(
            source, target, halo_send.at[k], halo_recv.at[k], device, MESH)

    halos_r = [
        halo(0, solid_view.at[1, :, 4:8], sol_left, right),
        halo(1, fine_view.at[:, 1, :, 4:8], from_left, right),
        halo(2, coarse_view.at[:, :, C - 1 : C], cfrom_left, right),
        halo(3, csolid_view.at[:, C - 1 : C], csol_left, right),
    ]
    halos_l = [
        halo(4, solid_view.at[0, :, 0:4], sol_right, left),
        halo(5, fine_view.at[:, 0, :, 0:4], from_right, left),
        halo(6, coarse_view.at[:, :, 0:1], cfrom_right, left),
        halo(7, csolid_view.at[:, 0:1], csol_right, left),
    ]
    pl.semaphore_wait(barrier, jnp.where(late, 1, groups))
    for copy in halos_r[:2]:
        copy.start()
    pl.semaphore_signal(ready, inc=1, device_id=right, device_id_type=MESH)
    for load in loads:
        load.start()

    def first_collision(f, s, start, rows, span):
        f = collide(f, s, tau_fine)
        for i in range(19):
            first[i, start : start + rows, span] = f[i]

    row = lax.broadcasted_iota(jnp.int32, (256, 128), 0)
    column = lax.broadcasted_iota(jnp.int32, (256, 128), 1)
    hit = (row // 32 == column // 16) & ((row % 16) // 2 == column % 8)
    boxes[...] = jnp.where(hit, 0.125, 0.0).astype(jnp.bfloat16)

    def second_collision(start, rows):
        low, high = streamed(first, start, rows)
        for f, h in ((low, 0), (high, 128)):
            span = slice(h, h + 128)
            f = collide(f, solid[start : start + rows, span], tau_fine)
            for i in range(19):
                second[i, start : start + rows, span] = f[i]

    def box_means(pair_sums):
        rest, parts = pair_sums, []
        for _ in range(3):
            piece = rest.astype(jnp.bfloat16).astype(F32)
            parts.append(piece)
            rest = rest - piece
        stacked = jnp.concatenate(parts, axis=0).astype(jnp.bfloat16)
        product = jnp.dot(stacked, boxes[...], preferred_element_type=F32)
        n = pair_sums.shape[0]
        return product[:n] + product[n : 2 * n] + product[2 * n :]

    def rescaled(means, rows):
        a = jnp.full((rows, 128), 1.0 - rescale, F32)
        keep = jnp.full((rows, 128), 0.5 * rescale, F32)
        return relaxed([means[rows * i : rows * i + rows, :] for i in range(19)], keep, keep, a)

    def near(rows):
        return lanes(rows) % 16 < 8

    def messages(which, buffer):
        return [
            pltpu.make_async_remote_copy(
                buffer.at[g], buffer.at[g], box_send.at[which, d], box_recv.at[which, g],
                peer, MESH)
            for d, peer in enumerate(peers)
        ]

    sends = [messages(0, inner), messages(1, outer_r), messages(2, outer_l)]

    def deliver(which):
        for send in sends[which]:
            send.start()

    def collect(which, buffer):
        for d, peer in enumerate(peers):
            pltpu.make_async_remote_copy(
                buffer.at[peer[0]], buffer.at[peer[0]], box_send.at[which, d],
                box_recv.at[which, peer[0]], peer, MESH).wait_recv()

    loads[0].wait()
    loads[1].wait()
    for t in range(X // 8):
        for h in HALVES:
            span = slice(h, h + 128)
            first_collision(
                [fine[i, 8 * t : 8 * t + 8, span] for i in range(19)],
                solid[PAD + 8 * t : PAD + 8 * t + 8, span], PAD + 8 * t, 8, span)
    for k, h in enumerate(HALVES):
        span = slice(h, h + 128)
        psolid[pl.ds(8 + k, 4, stride=2), :] = solid[PAD : PAD + 4, span]
        for i in range(19):
            pfirst[pl.ds(16 * i + 8 + k, 4, stride=2), :] = first[i, PAD : PAD + 4, span]
    for t in range(X // 8):
        second_collision(PAD + 8 * t, 8)
    for k, h in enumerate(HALVES):
        for i in range(19):
            psecond[pl.ds(16 * i + 10 + k, 2, stride=2), :] = second[
                i, PAD + 1 : PAD + 3, h : h + 128]
    for t in range(X // 8):
        low, high = streamed(second, PAD + 8 * t, 8)
        for i in range(19):
            moved[0, X * i + 8 * t : X * i + 8 * t + 8, :] = low[i]
            moved[1, X * i + 8 * t : X * i + 8 * t + 8, :] = high[i]
    sums = [
        moved[k, pl.ds(0, 152, stride=2), :] + moved[k, pl.ds(1, 152, stride=2), :]
        for k in range(2)
    ]
    f = rescaled(box_means(jnp.concatenate(sums, axis=1)), 8)
    for k in range(10):
        inner[g, k] = jnp.where(near(8), f[2 * k], f[min(2 * k + 1, 18)])

    @pl.when(jnp.logical_not(late))
    def _():
        deliver(0)

    for copy in halos_r[2:]:
        copy.start()

    pl.semaphore_wait(ready, 1)
    for copy in halos_l:
        copy.start()

    @pl.when(follows)
    def _():
        for device in peers:
            pl.semaphore_signal(lefts, inc=1, device_id=device, device_id_type=MESH)

    def beyond(halo, halo_solid, start):
        for k, h in enumerate(HALVES):
            span = slice(h, h + 128)
            s = halo_solid[k, :, 0, :]
            solid[start : start + 4, span] = s
            first_collision([halo[i, k, :, 0, :] for i in range(19)], s, start, 4, span)

    def restricted(sums, outer):
        means[...] = box_means(jnp.concatenate(sums, axis=1))
        f = rescaled(means, 2)
        for k in range(10):
            outer[g, 2 * k : 2 * k + 2, :] = jnp.where(near(2), f[2 * k], f[min(2 * k + 1, 18)])

    halos_l[0].wait_recv()
    halos_l[1].wait_recv()
    beyond(from_right, sol_right, PAD + X)
    second_collision(PAD + X - 1, 4)
    low, high = streamed(second, PAD + X - 2, 4)
    for k, values in enumerate((low, high)):
        for i in range(19):
            edge[k, 4 * i : 4 * i + 4, :] = values[i]
            moved[k, X * i + X - 2 : X * i + X, :] = values[i][0:2]
    restricted(
        [edge[k, pl.ds(0, 40, stride=2), :] + edge[k, pl.ds(1, 40, stride=2), :] for k in range(2)],
        outer_r)

    @pl.when(jnp.logical_not(late))
    def _():
        deliver(1)

    @pl.when(follows)
    def _():
        pl.semaphore_wait(lefts, groups - 1)
        pl.semaphore_signal(peers_in, inc=1, device_id=left, device_id_type=MESH)

    halos_r[0].wait_recv()
    halos_r[1].wait_recv()
    s = sol_left[...].reshape(8, 128)
    f = collide([from_left[i].reshape(8, 128) for i in range(19)], s, tau_fine)
    for k in range(2):
        psolid[pl.ds(k, 4, stride=2), :] = s[4 * k : 4 * k + 4]
        for i in range(19):
            pfirst[pl.ds(16 * i + k, 4, stride=2), :] = f[i][4 * k : 4 * k + 4]
    f = collide(packed(pfirst, 2), psolid[2:10, :], tau_fine)
    for i in range(19):
        psecond[16 * i + 2 : 16 * i + 10, :] = f[i]
    f = packed(psecond, 4)
    for i in range(19):
        pmoved[8 * i : 8 * i + 8, :] = f[i]
    restricted(
        [pmoved[pl.ds(k, 40, stride=4), :] + pmoved[pl.ds(k + 2, 40, stride=4), :]
         for k in range(2)],
        outer_l)

    @pl.when(late)
    def _():
        pl.semaphore_wait(peers_in, 1)
        deliver(0)
        deliver(1)

    deliver(2)
    for k in range(2):
        for i in range(19):
            moved[k, X * i : X * i + 2, :] = pmoved[pl.ds(8 * i + 4 + k, 2, stride=2), :]

    loads[4].wait()
    sources, present = [], []
    for q in range(4):
        source = jnp.int32(0)
        found = jnp.int32(0)
        for k in range(groups):
            match = (slot_ref[k] == 4 * g + q).astype(jnp.int32)
            source = jnp.maximum(source, k * match)
            found = jnp.maximum(found, match)
        sources.append(source)
        present.append(found)

    def pasted(half, rows, tile, start):
        span = slice(128 * half, 128 * half + 128)
        one, two = sources[2 * half], sources[2 * half + 1]
        close = near(rows)
        put = jnp.where(
            close,
            jnp.full((rows, 128), present[2 * half], jnp.int32),
            jnp.full((rows, 128), present[2 * half + 1], jnp.int32),
        ) > 0
        f = []
        for k in range(10):
            tile_one, tile_two = tile(one, k), tile(two, k)
            i = 2 * k
            value = jnp.where(close, tile_one, pltpu.roll(tile_two, 8, 1))
            f.append(jnp.where(put, value, coarse[i, start : start + rows, span]))
            if i + 1 < 19:
                value = jnp.where(close, pltpu.roll(tile_one, 120, 1), tile_two)
                f.append(jnp.where(put, value, coarse[i + 1, start : start + rows, span]))
        return collide(f, csolid[start : start + rows, span], tau_coarse), span

    def cbeyond(halo, halo_solid, start):
        for k, h in enumerate(HALVES):
            span = slice(h, h + 128)
            csolid[start : start + 1, span] = halo_solid[k, :, 0, :]
            for i in range(19):
                coarse[i, start : start + 1, span] = halo[i, k, :, 0, :]

    loads[2].wait()
    loads[3].wait()
    halos_l[2].wait_recv()
    halos_l[3].wait_recv()
    cbeyond(cfrom_right, csol_right, PAD + C)
    collect(0, inner)
    for half in range(2):
        f, span = pasted(half, C, lambda source, k: inner[source, k], PAD)
        for i in range(19):
            settled[i, 1 : 1 + C, span] = f[i]

    collect(1, outer_r)
    for half in range(2):
        f, span = pasted(
            half, 2, lambda source, k: outer_r[source, 2 * k : 2 * k + 2, :], PAD + C - 1)
        for i in range(19):
            settled[i, C : C + 2, span] = f[i]

    halos_r[2].wait_recv()
    halos_r[3].wait_recv()
    cbeyond(cfrom_left, csol_left, PAD - 1)
    for copy in halos_r + halos_l + sends[0] + sends[1]:
        copy.wait_send()
    collect(2, outer_l)
    for half in range(2):
        f, span = pasted(
            half, 2, lambda source, k: outer_l[source, 2 * k : 2 * k + 2, :], PAD - 1)
        for i in range(19):
            settled[i, 0:2, span] = f[i]

    for copy in sends[2]:
        copy.wait_send()


def finish(moved, settled, fine_out, coarse_out, cmoved, store_sem):
    stores = [
        pltpu.make_async_copy(moved.at[k], fine_out.at[0, :, :, h : h + 128], store_sem.at[k])
        for k, h in enumerate(HALVES)
    ]
    for store in stores:
        store.start()
    low, high = streamed(settled, 1, C)
    for i in range(19):
        cmoved[i, :, 0:128] = low[i]
        cmoved[i, :, 128:256] = high[i]
    stores.append(pltpu.make_async_copy(cmoved, coarse_out.at[0], store_sem.at[2]))
    stores[2].start()
    for store in stores:
        store.wait()


def solution(mesh):
    groups, blocks = mesh.shape["grp"], mesh.shape["blk"]
    vmem = pl.BlockSpec(memory_space=pltpu.VMEM)
    hbm = pl.BlockSpec(memory_space=pltpu.HBM)

    def planes(x, *leading):
        n = len(leading)
        order = tuple(range(n)) + (n + 1, n, n + 2)
        x = x.reshape(leading + (8, 2, 128)).transpose(order)
        return x.reshape(leading + (2, 8, 1, 128))

    def per_device(fine_pops, fine_solid, coarse_pops, coarse_solid, coarse_slot):
        body = lambda *refs: kernel(groups, blocks, *refs)
        moved, settled = pl.pallas_call(
            body,
            out_shape=(
                jax.ShapeDtypeStruct((2, 19 * X, 128), F32),
                jax.ShapeDtypeStruct((19, 2 * C, 256), F32),
            ),
            in_specs=[hbm] * 9,
            out_specs=(vmem, vmem),
            scratch_shapes=[
                pltpu.VMEM((19, X, 256), F32),
                pltpu.VMEM((X + 2 * PAD, 256), F32),
                pltpu.VMEM((19, C + 2 * PAD, 256), F32),
                pltpu.VMEM((C + 2 * PAD, 256), F32),
                pltpu.VMEM((19, X + 2 * PAD, 256), F32),
                pltpu.VMEM((19, X + 2 * PAD, 256), F32),
                pltpu.VMEM((2, 80, 128), F32),
                pltpu.VMEM((19 * 16, 128), F32),
                pltpu.VMEM((19 * 16, 128), F32),
                pltpu.VMEM((16, 128), F32),
                pltpu.VMEM((160, 128), F32),
                pltpu.VMEM((40, 128), F32),
                pltpu.VMEM((256, 128), jnp.bfloat16),
                pltpu.VMEM((groups, 10, 8, 128), F32),
                pltpu.VMEM((groups, 24, 128), F32),
                pltpu.VMEM((groups, 24, 128), F32),
            ]
            + [pltpu.VMEM((19, 2, 4, 1, 128), F32)] * 2
            + [pltpu.VMEM((2, 4, 1, 128), F32)] * 2
            + [pltpu.VMEM((19, 2, 1, 1, 128), F32)] * 2
            + [pltpu.VMEM((2, 1, 1, 128), F32)] * 2
            + [
                pltpu.SMEM((groups,), jnp.int32),
                pltpu.SemaphoreType.DMA((5,)),
                pltpu.SemaphoreType.REGULAR,
                pltpu.SemaphoreType.REGULAR,
                pltpu.SemaphoreType.REGULAR,
                pltpu.SemaphoreType.DMA((8,)),
                pltpu.SemaphoreType.DMA((8,)),
                pltpu.SemaphoreType.DMA((3, groups)),
                pltpu.SemaphoreType.DMA((3, groups)),
            ],
            compiler_params=pltpu.CompilerParams(
                collective_id=0, has_side_effects=True, vmem_limit_bytes=16 << 20),
        )(*[
            pltpu.with_memory_space_constraint(x, pltpu.HBM)
            for x in (
                coarse_slot, fine_pops, fine_solid, coarse_pops, coarse_solid,
                planes(fine_pops, 19, 2), planes(fine_solid, 2),
                planes(coarse_pops, 19), planes(coarse_solid),
            )
        ])
        return pl.pallas_call(
            finish,
            out_shape=(
                jax.ShapeDtypeStruct(fine_pops.shape, F32),
                jax.ShapeDtypeStruct(coarse_pops.shape, F32),
            ),
            in_specs=[vmem, vmem],
            out_specs=(hbm, hbm),
            scratch_shapes=[pltpu.VMEM((19, C, 256), F32), pltpu.SemaphoreType.DMA((3,))],
            compiler_params=pltpu.CompilerParams(vmem_limit_bytes=4 << 20),
        )(moved.reshape(2, 19, X, 128), settled)

    placed = (
        P("grp", None, "blk", None),
        P("grp", "blk", None),
        P("grp", None, "blk", None),
        P("grp", "blk", None),
        P(),
    )
    return jax.shard_map(
        per_device,
        mesh=mesh,
        in_specs=placed,
        out_specs=(P("grp", None, "blk", None), P("grp", None, "blk", None)),
        check_vma=False,
    )
```

```python
import jax
import jax.numpy as jnp
import numpy as np
from jax import lax
from jax.experimental import pallas as pl
from jax.experimental.pallas import tpu as pltpu
from jax.sharding import PartitionSpec as P

MESH = pl.DeviceIdType.MESH
F32 = jnp.float32

lattice_vel = [
    (0, 0, 0), (1, 0, 0), (-1, 0, 0), (0, 1, 0), (0, -1, 0), (0, 0, 1), (0, 0, -1),
    (1, 1, 0), (-1, -1, 0), (1, -1, 0), (-1, 1, 0), (1, 0, 1), (-1, 0, -1),
    (1, 0, -1), (-1, 0, 1), (0, 1, 1), (0, -1, -1), (0, 1, -1), (0, -1, 1),
]
tau_fine = 0.6
tau_coarse = 0.55
rescale = 2.0 * tau_coarse / tau_fine
RIGHT = [i for i in range(19) if lattice_vel[i][0] == 1]
LEFT = [i for i in range(19) if lattice_vel[i][0] == -1]
STAY = [i for i in range(19) if lattice_vel[i][0] == 0]
X = 16
C = 8
ROW = 12
PAD = 8
HALVES = (0, 128)


def total(terms):
    while len(terms) > 1:
        terms = [a + b for a, b in zip(terms[::2], terms[1::2])] + terms[len(terms) // 2 * 2 :]
    return terms[0]


def relaxed(f, keep_even, keep_odd, a):
    even = [None] * 19
    odd = [None] * 19
    for i in range(1, 19, 2):
        even[i] = f[i] + f[i + 1]
        odd[i] = f[i] - f[i + 1]
    rho = total([f[0]] + [even[i] for i in range(1, 19, 2)])
    j = []
    for axis in range(3):
        plus = [odd[i] for i in range(1, 19, 2) if lattice_vel[i][axis] > 0]
        minus = [odd[i] for i in range(1, 19, 2) if lattice_vel[i][axis] < 0]
        j.append(total(plus) - total(minus) if minus else total(plus))
    inverse = 1.0 / rho
    q = a * inverse
    jj = j[0] * j[0] + j[1] * j[1] + j[2] * j[2]
    base = a * rho - (1.5 * q) * jj
    out = [None] * 19
    out[0] = 2.0 * keep_even * f[0] + (1.0 / 3.0) * base
    axis_base = (1.0 / 18.0) * base
    edge_base = (1.0 / 36.0) * base
    axis_q = (4.5 / 18.0) * q
    edge_q = (4.5 / 36.0) * q
    axis_a = (3.0 / 18.0) * a
    edge_a = (3.0 / 36.0) * a
    for i in range(1, 19, 2):
        cj = None
        for axis in range(3):
            c = lattice_vel[i][axis]
            if c:
                if cj is None:
                    cj = j[axis] if c > 0 else -j[axis]
                else:
                    cj = cj + j[axis] if c > 0 else cj - j[axis]
        if i < 7:
            e = axis_base + axis_q * (cj * cj) + keep_even * even[i]
            o = axis_a * cj + keep_odd * odd[i]
        else:
            e = edge_base + edge_q * (cj * cj) + keep_even * even[i]
            o = edge_a * cj + keep_odd * odd[i]
        out[i] = e + o
        out[i + 1] = e - o
    return out


def collide(f, solid, tau):
    a = (1.0 - solid) * (1.0 / tau)
    keep_even = 0.5 * (1.0 - a)
    return relaxed(f, keep_even, keep_even - solid, a)


def lane_shift(low, high, cy, cz, lane):
    if cy == 0 and cz == 0:
        return low, high
    shift = 16 * cy + cz
    parts = []
    for v in (low, high):
        moved = pltpu.roll(v, shift % 128, 1)
        if cz:
            wrapped = pltpu.roll(v, (shift - 16 * cz) % 128, 1)
            z = lane % 16
            moved = jnp.where(z == (0 if cz > 0 else 15), wrapped, moved)
        parts.append(moved)
    if cy == 0:
        return parts[0], parts[1]
    crossing = lane < 16 if cy > 0 else lane >= 112
    return jnp.where(crossing, parts[1], parts[0]), jnp.where(crossing, parts[0], parts[1])


def lanes(rows):
    return lax.broadcasted_iota(jnp.int32, (rows, 128), 1)


def streamed(source, row, rows):
    lane = lanes(rows)
    low, high = [], []
    for i in range(19):
        cx, cy, cz = lattice_vel[i]
        start = row - cx
        a = source[i, start : start + rows, 0:128]
        b = source[i, start : start + rows, 128:256]
        a, b = lane_shift(a, b, cy, cz, lane)
        low.append(a)
        high.append(b)
    return low, high


def packed(source, row):
    lane = lanes(8)
    odd = lax.broadcasted_iota(jnp.int32, (8, 128), 0) % 2 == 1
    out = []
    for i in range(19):
        cx, cy, cz = lattice_vel[i]
        start = 16 * i + row - 2 * cx
        v = source[start : start + 8, :]
        if cy or cz:
            shift = 16 * cy + cz
            m = pltpu.roll(v, shift % 128, 1)
            if cz:
                wrapped = pltpu.roll(v, (shift - 16 * cz) % 128, 1)
                m = jnp.where(lane % 16 == (0 if cz > 0 else 15), wrapped, m)
            if cy:
                other = jnp.where(odd, pltpu.roll(m, 1, 0), pltpu.roll(m, 7, 0))
                m = jnp.where(lane < 16 if cy > 0 else lane >= 112, other, m)
            v = m
        out.append(v)
    return out


def kernel(
    groups, blocks, slot_hbm, fine_hbm, solid_hbm, coarse_hbm, csolid_hbm,
    fine_view, solid_view, coarse_view, csolid_view, moved, settled,
    fine, solid, coarse, csolid, first, second, edge, pfirst, psecond, psolid, pmoved, means, boxes, inner, outer_r, outer_l,
    from_left, from_right, sol_left, sol_right, cfrom_left, cfrom_right, csol_left, csol_right,
    slot_ref, load_sem, ready, lefts, peers_in, halo_send, halo_recv, box_send, box_recv,
):
    g = lax.axis_index("grp")
    b = lax.axis_index("blk")
    right = (g, lax.rem(b + 1, blocks))
    left = (g, lax.rem(b + blocks - 1, blocks))
    half = groups // 2
    place = jnp.where(lax.rem(g, 2) == 1, g // 2, half + lax.rem(g // 2 + half - 1, half))
    peers = []
    for k in range(groups - 1):
        k = k + (place <= k).astype(jnp.int32)
        peers.append((jnp.where(k < half, 2 * k + 1, lax.rem(2 * (k - half) + 2, groups)), b))

    late = lax.rem(b, ROW) == ROW - 1
    follows = lax.rem(b, ROW) == 0

    barrier = pltpu.get_barrier_semaphore()
    pl.semaphore_signal(barrier, inc=1, device_id=left, device_id_type=MESH)

    @pl.when(jnp.logical_not(late))
    def _():
        for device in peers:
            pl.semaphore_signal(barrier, inc=1, device_id=device, device_id_type=MESH)

    loads = [
        pltpu.make_async_copy(solid_hbm.at[0], solid.at[PAD : PAD + X], load_sem.at[0]),
        pltpu.make_async_copy(fine_hbm.at[0], fine, load_sem.at[1]),
        pltpu.make_async_copy(csolid_hbm.at[0], csolid.at[PAD : PAD + C], load_sem.at[2]),
        pltpu.make_async_copy(coarse_hbm.at[0], coarse.at[:, PAD : PAD + C], load_sem.at[3]),
        pltpu.make_async_copy(slot_hbm, slot_ref, load_sem.at[4]),
    ]

    def halo(k, source, target, device):
        return pltpu.make_async_remote_copy(
            source, target, halo_send.at[k], halo_recv.at[k], device, MESH)

    halos_r = [
        halo(0, solid_view.at[1, :, 4:8], sol_left, right),
        halo(1, fine_view.at[:, 1, :, 4:8], from_left, right),
        halo(2, coarse_view.at[:, :, C - 1 : C], cfrom_left, right),
        halo(3, csolid_view.at[:, C - 1 : C], csol_left, right),
    ]
    halos_l = [
        halo(4, solid_view.at[0, :, 0:4], sol_right, left),
        halo(5, fine_view.at[:, 0, :, 0:4], from_right, left),
        halo(6, coarse_view.at[:, :, 0:1], cfrom_right, left),
        halo(7, csolid_view.at[:, 0:1], csol_right, left),
    ]
    pl.semaphore_wait(barrier, jnp.where(late, 1, groups))
    for copy in halos_r[:2]:
        copy.start()
    pl.semaphore_signal(ready, inc=1, device_id=right, device_id_type=MESH)
    for load in loads:
        load.start()

    def first_collision(f, s, start, rows, span):
        f = collide(f, s, tau_fine)
        for i in range(19):
            first[i, start : start + rows, span] = f[i]

    row = lax.broadcasted_iota(jnp.int32, (256, 128), 0)
    column = lax.broadcasted_iota(jnp.int32, (256, 128), 1)
    hit = (row // 32 == column // 16) & ((row % 16) // 2 == column % 8)
    boxes[...] = jnp.where(hit, 0.125, 0.0).astype(jnp.bfloat16)

    def second_collision(start, rows):
        low, high = streamed(first, start, rows)
        for f, h in ((low, 0), (high, 128)):
            span = slice(h, h + 128)
            f = collide(f, solid[start : start + rows, span], tau_fine)
            for i in range(19):
                second[i, start : start + rows, span] = f[i]

    def box_means(pair_sums):
        rest, parts = pair_sums, []
        for _ in range(3):
            piece = rest.astype(jnp.bfloat16).astype(F32)
            parts.append(piece)
            rest = rest - piece
        stacked = jnp.concatenate(parts, axis=0).astype(jnp.bfloat16)
        product = jnp.dot(stacked, boxes[...], preferred_element_type=F32)
        n = pair_sums.shape[0]
        return product[:n] + product[n : 2 * n] + product[2 * n :]

    def rescaled(means, rows):
        a = jnp.full((rows, 128), 1.0 - rescale, F32)
        keep = jnp.full((rows, 128), 0.5 * rescale, F32)
        return relaxed([means[rows * i : rows * i + rows, :] for i in range(19)], keep, keep, a)

    def near(rows):
        return lanes(rows) % 16 < 8

    def messages(which, buffer):
        return [
            pltpu.make_async_remote_copy(
                buffer.at[g], buffer.at[g], box_send.at[which], box_recv.at[which], peer, MESH)
            for peer in peers
        ]

    def whole(which, buffer):
        span = buffer.at[0 : groups - 1]
        return pltpu.make_async_remote_copy(
            span, span, box_send.at[which], box_recv.at[which], peers[0], MESH)

    sends = [messages(0, inner), messages(1, outer_r), messages(2, outer_l)]

    def deliver(which):
        for send in sends[which]:
            send.start()

    def collect(which, buffer):
        whole(which, buffer).wait_recv()

    loads[0].wait()
    loads[1].wait()
    for t in range(X // 8):
        for h in HALVES:
            span = slice(h, h + 128)
            first_collision(
                [fine[i, 8 * t : 8 * t + 8, span] for i in range(19)],
                solid[PAD + 8 * t : PAD + 8 * t + 8, span], PAD + 8 * t, 8, span)
    for k, h in enumerate(HALVES):
        span = slice(h, h + 128)
        psolid[pl.ds(8 + k, 4, stride=2), :] = solid[PAD : PAD + 4, span]
        for i in range(19):
            pfirst[pl.ds(16 * i + 8 + k, 4, stride=2), :] = first[i, PAD : PAD + 4, span]
    for t in range(X // 8):
        second_collision(PAD + 8 * t, 8)
    for k, h in enumerate(HALVES):
        for i in range(19):
            psecond[pl.ds(16 * i + 10 + k, 2, stride=2), :] = second[
                i, PAD + 1 : PAD + 3, h : h + 128]
    for t in range(X // 8):
        low, high = streamed(second, PAD + 8 * t, 8)
        for i in range(19):
            moved[0, X * i + 8 * t : X * i + 8 * t + 8, :] = low[i]
            moved[1, X * i + 8 * t : X * i + 8 * t + 8, :] = high[i]
    sums = [
        moved[k, pl.ds(0, 152, stride=2), :] + moved[k, pl.ds(1, 152, stride=2), :]
        for k in range(2)
    ]
    f = rescaled(box_means(jnp.concatenate(sums, axis=1)), 8)
    for k in range(10):
        inner[g, k] = jnp.where(near(8), f[2 * k], f[min(2 * k + 1, 18)])

    @pl.when(jnp.logical_not(late))
    def _():
        deliver(0)

    for copy in halos_r[2:]:
        copy.start()

    pl.semaphore_wait(ready, 1)
    for copy in halos_l:
        copy.start()

    @pl.when(follows)
    def _():
        for device in peers:
            pl.semaphore_signal(lefts, inc=1, device_id=device, device_id_type=MESH)

    def beyond(halo, halo_solid, start):
        for k, h in enumerate(HALVES):
            span = slice(h, h + 128)
            s = halo_solid[k, :, 0, :]
            solid[start : start + 4, span] = s
            first_collision([halo[i, k, :, 0, :] for i in range(19)], s, start, 4, span)

    def restricted(sums, outer):
        means[...] = box_means(jnp.concatenate(sums, axis=1))
        f = rescaled(means, 2)
        for k in range(10):
            outer[g, 2 * k : 2 * k + 2, :] = jnp.where(near(2), f[2 * k], f[min(2 * k + 1, 18)])

    halos_l[0].wait_recv()
    halos_l[1].wait_recv()
    beyond(from_right, sol_right, PAD + X)
    second_collision(PAD + X - 1, 4)
    low, high = streamed(second, PAD + X - 2, 4)
    for k, values in enumerate((low, high)):
        for i in range(19):
            edge[k, 4 * i : 4 * i + 4, :] = values[i]
            moved[k, X * i + X - 2 : X * i + X, :] = values[i][0:2]
    restricted(
        [edge[k, pl.ds(0, 40, stride=2), :] + edge[k, pl.ds(1, 40, stride=2), :] for k in range(2)],
        outer_r)

    @pl.when(jnp.logical_not(late))
    def _():
        deliver(1)

    @pl.when(follows)
    def _():
        pl.semaphore_wait(lefts, groups - 1)
        pl.semaphore_signal(peers_in, inc=1, device_id=left, device_id_type=MESH)

    halos_r[0].wait_recv()
    halos_r[1].wait_recv()
    s = sol_left[...].reshape(8, 128)
    f = collide([from_left[i].reshape(8, 128) for i in range(19)], s, tau_fine)
    for k in range(2):
        psolid[pl.ds(k, 4, stride=2), :] = s[4 * k : 4 * k + 4]
        for i in range(19):
            pfirst[pl.ds(16 * i + k, 4, stride=2), :] = f[i][4 * k : 4 * k + 4]
    f = collide(packed(pfirst, 2), psolid[2:10, :], tau_fine)
    for i in range(19):
        psecond[16 * i + 2 : 16 * i + 10, :] = f[i]
    f = packed(psecond, 4)
    for i in range(19):
        pmoved[8 * i : 8 * i + 8, :] = f[i]
    restricted(
        [pmoved[pl.ds(k, 40, stride=4), :] + pmoved[pl.ds(k + 2, 40, stride=4), :]
         for k in range(2)],
        outer_l)

    @pl.when(late)
    def _():
        pl.semaphore_wait(peers_in, 1)
        deliver(0)
        deliver(1)

    deliver(2)
    for k in range(2):
        for i in range(19):
            moved[k, X * i : X * i + 2, :] = pmoved[pl.ds(8 * i + 4 + k, 2, stride=2), :]

    loads[4].wait()
    sources, present = [], []
    for q in range(4):
        source = jnp.int32(0)
        found = jnp.int32(0)
        for k in range(groups):
            match = (slot_ref[k] == 4 * g + q).astype(jnp.int32)
            source = jnp.maximum(source, k * match)
            found = jnp.maximum(found, match)
        sources.append(source)
        present.append(found)

    def pasted(half, rows, tile, start):
        span = slice(128 * half, 128 * half + 128)
        one, two = sources[2 * half], sources[2 * half + 1]
        close = near(rows)
        put = jnp.where(
            close,
            jnp.full((rows, 128), present[2 * half], jnp.int32),
            jnp.full((rows, 128), present[2 * half + 1], jnp.int32),
        ) > 0
        f = []
        for k in range(10):
            tile_one, tile_two = tile(one, k), tile(two, k)
            i = 2 * k
            value = jnp.where(close, tile_one, pltpu.roll(tile_two, 8, 1))
            f.append(jnp.where(put, value, coarse[i, start : start + rows, span]))
            if i + 1 < 19:
                value = jnp.where(close, pltpu.roll(tile_one, 120, 1), tile_two)
                f.append(jnp.where(put, value, coarse[i + 1, start : start + rows, span]))
        return collide(f, csolid[start : start + rows, span], tau_coarse), span

    def cbeyond(halo, halo_solid, start):
        for k, h in enumerate(HALVES):
            span = slice(h, h + 128)
            csolid[start : start + 1, span] = halo_solid[k, :, 0, :]
            for i in range(19):
                coarse[i, start : start + 1, span] = halo[i, k, :, 0, :]

    loads[2].wait()
    loads[3].wait()
    halos_l[2].wait_recv()
    halos_l[3].wait_recv()
    cbeyond(cfrom_right, csol_right, PAD + C)
    collect(0, inner)
    for half in range(2):
        f, span = pasted(half, C, lambda source, k: inner[source, k], PAD)
        for i in range(19):
            settled[i, 1 : 1 + C, span] = f[i]

    collect(1, outer_r)
    for half in range(2):
        f, span = pasted(
            half, 2, lambda source, k: outer_r[source, 2 * k : 2 * k + 2, :], PAD + C - 1)
        for i in range(19):
            settled[i, C : C + 2, span] = f[i]

    halos_r[2].wait_recv()
    halos_r[3].wait_recv()
    cbeyond(cfrom_left, csol_left, PAD - 1)
    for copy in halos_r + halos_l + [whole(0, inner), whole(1, outer_r)]:
        copy.wait_send()
    collect(2, outer_l)
    for half in range(2):
        f, span = pasted(
            half, 2, lambda source, k: outer_l[source, 2 * k : 2 * k + 2, :], PAD - 1)
        for i in range(19):
            settled[i, 0:2, span] = f[i]

    whole(2, outer_l).wait_send()


def finish(moved, settled, fine_out, coarse_out, cmoved, store_sem):
    stores = [
        pltpu.make_async_copy(moved.at[k], fine_out.at[0, :, :, h : h + 128], store_sem.at[k])
        for k, h in enumerate(HALVES)
    ]
    for store in stores:
        store.start()
    low, high = streamed(settled, 1, C)
    for i in range(19):
        cmoved[i, :, 0:128] = low[i]
        cmoved[i, :, 128:256] = high[i]
    stores.append(pltpu.make_async_copy(cmoved, coarse_out.at[0], store_sem.at[2]))
    stores[2].start()
    for store in stores:
        store.wait()


def solution(mesh):
    groups, blocks = mesh.shape["grp"], mesh.shape["blk"]
    vmem = pl.BlockSpec(memory_space=pltpu.VMEM)
    hbm = pl.BlockSpec(memory_space=pltpu.HBM)

    def planes(x, *leading):
        n = len(leading)
        order = tuple(range(n)) + (n + 1, n, n + 2)
        x = x.reshape(leading + (8, 2, 128)).transpose(order)
        return x.reshape(leading + (2, 8, 1, 128))

    def per_device(fine_pops, fine_solid, coarse_pops, coarse_solid, coarse_slot):
        body = lambda *refs: kernel(groups, blocks, *refs)
        moved, settled = pl.pallas_call(
            body,
            out_shape=(
                jax.ShapeDtypeStruct((2, 19 * X, 128), F32),
                jax.ShapeDtypeStruct((19, 2 * C, 256), F32),
            ),
            in_specs=[hbm] * 9,
            out_specs=(vmem, vmem),
            scratch_shapes=[
                pltpu.VMEM((19, X, 256), F32),
                pltpu.VMEM((X + 2 * PAD, 256), F32),
                pltpu.VMEM((19, C + 2 * PAD, 256), F32),
                pltpu.VMEM((C + 2 * PAD, 256), F32),
                pltpu.VMEM((19, X + 2 * PAD, 256), F32),
                pltpu.VMEM((19, X + 2 * PAD, 256), F32),
                pltpu.VMEM((2, 80, 128), F32),
                pltpu.VMEM((19 * 16, 128), F32),
                pltpu.VMEM((19 * 16, 128), F32),
                pltpu.VMEM((16, 128), F32),
                pltpu.VMEM((160, 128), F32),
                pltpu.VMEM((40, 128), F32),
                pltpu.VMEM((256, 128), jnp.bfloat16),
                pltpu.VMEM((groups, 10, 8, 128), F32),
                pltpu.VMEM((groups, 24, 128), F32),
                pltpu.VMEM((groups, 24, 128), F32),
            ]
            + [pltpu.VMEM((19, 2, 4, 1, 128), F32)] * 2
            + [pltpu.VMEM((2, 4, 1, 128), F32)] * 2
            + [pltpu.VMEM((19, 2, 1, 1, 128), F32)] * 2
            + [pltpu.VMEM((2, 1, 1, 128), F32)] * 2
            + [
                pltpu.SMEM((groups,), jnp.int32),
                pltpu.SemaphoreType.DMA((5,)),
                pltpu.SemaphoreType.REGULAR,
                pltpu.SemaphoreType.REGULAR,
                pltpu.SemaphoreType.REGULAR,
                pltpu.SemaphoreType.DMA((8,)),
                pltpu.SemaphoreType.DMA((8,)),
                pltpu.SemaphoreType.DMA((3,)),
                pltpu.SemaphoreType.DMA((3,)),
            ],
            compiler_params=pltpu.CompilerParams(
                collective_id=0, has_side_effects=True, vmem_limit_bytes=16 << 20),
        )(*[
            pltpu.with_memory_space_constraint(x, pltpu.HBM)
            for x in (
                coarse_slot, fine_pops, fine_solid, coarse_pops, coarse_solid,
                planes(fine_pops, 19, 2), planes(fine_solid, 2),
                planes(coarse_pops, 19), planes(coarse_solid),
            )
        ])
        return pl.pallas_call(
            finish,
            out_shape=(
                jax.ShapeDtypeStruct(fine_pops.shape, F32),
                jax.ShapeDtypeStruct(coarse_pops.shape, F32),
            ),
            in_specs=[vmem, vmem],
            out_specs=(hbm, hbm),
            scratch_shapes=[pltpu.VMEM((19, C, 256), F32), pltpu.SemaphoreType.DMA((3,))],
            compiler_params=pltpu.CompilerParams(vmem_limit_bytes=4 << 20),
        )(moved.reshape(2, 19, X, 128), settled)

    placed = (
        P("grp", None, "blk", None),
        P("grp", "blk", None),
        P("grp", None, "blk", None),
        P("grp", "blk", None),
        P(),
    )
    return jax.shard_map(
        per_device,
        mesh=mesh,
        in_specs=placed,
        out_specs=(P("grp", None, "blk", None), P("grp", None, "blk", None)),
        check_vma=False,
    )
```
